256 devices in a mesh: mem: 32 (over y, x, core), cell: 8 (over z).
Axes of the slice: x: 4, y: 4, z: 8, core: 2. Of those that a mesh axis runs over, the one named last changes fastest.
Arguments:
- prior_ensemble: bfloat16 [512, 2, 262144], P('mem', None, 'cell'), may hold values from -12 to 12
- measurement_location: int32 [32, 4096], P('cell', 'mem'), may hold values from 0 to 524287, as said below
- measurement_datum: float32 [32, 4096], P('cell', 'mem'), may hold values from -32 to 32
- measurement_spread: float32 [32, 4096], P('cell', 'mem'), may hold values from 1.2 to 20
Outputs:
- analysis: bfloat16 [512, 2, 262144], P('mem', None, 'cell')
The draws below stay inside these ranges and needn't reach their ends.
Inputs may be any that keep to these rules, and one draw needn't show every extreme that they name: `measurement_location`: with v an entry at row r and column c, v // 262144 is its field and v % 262144 its cell; that cell is one of the 1024 cells that begin at ((r // 4) * 32 + c // 128) * 1024. Within each such block of 4 rows and 128 columns the entries are distinct, and they include the first cell of field 0 and the last cell of field 1 of that range.
All inputs are finite; a program needn't handle non-finite values.
Results may differ from the reference program's by a relative error of at most 0.0063.
Values may be sent and summed in bfloat16 or wider, within the bound.
No kernel may reach another device: no remote copies, remote signals or barrier semaphores. Data moves between devices by JAX's collectives and lax.ppermute only.
A program may use at most 64 MiB of HBM per device.

```python
import math
import jax
import jax.numpy as jnp
from jax import lax

M = 512
GRID_SHARE_SPAN = 1024
OBS_ROWS = 4
NS_ITERS = 8
CELLS = 262144
OBS_R = 32
OBS_C = 4096
N_MEM = 32
N_CELL = 8


def draw_prior_ensemble(key, part):
    keys = jax.random.split(key, 7)
    pattern_count = 24
    base = jax.random.normal(keys[0], (1, 2, CELLS), jnp.float32)
    cell_scale = jnp.exp(jax.random.uniform(keys[1], (1, 2, CELLS), jnp.float32, math.log(0.5), math.log(2.0)))
    patterns = jax.random.normal(keys[2], (pattern_count, 2, CELLS), jnp.float32)
    strength = jnp.exp(jax.random.uniform(keys[3], (pattern_count,), jnp.float32, math.log(0.06), math.log(0.25)))
    member_scale = jnp.exp(jax.random.uniform(keys[5], (M, 1, 1), jnp.float32, math.log(0.15), math.log(0.6)))
    coefs = jax.random.normal(keys[4], (M, pattern_count), jnp.float32)
    noise = jax.random.normal(keys[6], (M, 2, CELLS), jnp.float32)
    signal = member_scale * noise
    for index in range(pattern_count):
        signal = signal + (coefs[:, index] * strength[index])[:, None, None] * patterns[index][None, :, :]
    return jnp.clip(base + cell_scale * signal, -12.0, 12.0).astype(jnp.bfloat16)


def draw_measurement_location(key, part):
    block_count = N_MEM * N_CELL
    obs_dev = OBS_ROWS * 128
    keys = jax.random.split(jax.random.fold_in(key, 17), block_count)

    def one_block(block_key):
        key_inner, key_order = jax.random.split(block_key)
        inner = jax.random.permutation(key_inner, 2 * GRID_SHARE_SPAN - 2)[:obs_dev - 2].astype(jnp.int32) + 1
        chosen = jnp.concatenate([jnp.array([0, 2 * GRID_SHARE_SPAN - 1], jnp.int32), inner])
        return jax.random.permutation(key_order, chosen)
    slot_table = jax.vmap(one_block)(keys)
    block_id = jnp.arange(block_count, dtype=jnp.int32)[:, None]
    cell_ids = slot_table // GRID_SHARE_SPAN * CELLS + block_id * GRID_SHARE_SPAN + slot_table % GRID_SHARE_SPAN
    cell_ids = cell_ids.reshape(N_CELL, N_MEM, OBS_ROWS, 128).transpose(0, 2, 1, 3)
    return cell_ids.reshape(OBS_ROWS * N_CELL, 128 * N_MEM).astype(jnp.int32)


def draw_measurement_spread(key, part):
    keys = jax.random.split(jax.random.fold_in(key, 29), 2)
    block_count = N_MEM * N_CELL
    base = jnp.exp(jax.random.uniform(keys[0], (N_CELL, OBS_ROWS, N_MEM, 128), jnp.float32, math.log(4.0), math.log(20.0)))
    heavy_ids = jax.random.permutation(keys[1], block_count)[:2]
    block_ids = jnp.arange(block_count, dtype=jnp.int32)
    heavy = jnp.any(block_ids[:, None] == heavy_ids[None, :], axis=1)
    factor = jnp.where(heavy, 0.3, 1.0).astype(jnp.float32).reshape(N_CELL, 1, N_MEM, 1)
    return (base * factor).reshape(OBS_ROWS * N_CELL, 128 * N_MEM).astype(jnp.float32)


def steps_of(rng, extent, shards, low, largest):
    gain, own = 1.0, jax.random.fold_in(rng, 6)
    for dim, shards_of in shards:
        steps = jnp.exp(jax.random.uniform(jax.random.fold_in(own, dim), (shards_of,), jnp.float32, low / len(shards), largest / len(shards)))
        gain = gain * jnp.repeat(steps, extent[dim] // shards_of).reshape([-1 if axis == dim else 1 for axis in range(len(extent))])
    return gain


def normal_values(rng, shape, scale, reach, pieces=(), held_as=jnp.bfloat16):
    values = scale * jax.random.normal(rng, shape, jnp.float32)
    if pieces:
        values = values * steps_of(rng, shape, pieces, -0.22, 0.18)
    return jnp.clip(values, -reach, reach).astype(held_as)


def setup_inputs(seed: int = 0) -> dict:
    streams_of = jax.random.split(jax.random.key(seed), 5)
    return {
        "prior_ensemble": draw_prior_ensemble(jax.random.fold_in(streams_of[4], 71), 0),
        "measurement_location": draw_measurement_location(jax.random.fold_in(streams_of[4], 71), 0),
        "measurement_datum": normal_values(streams_of[2], (OBS_R, OBS_C), 8.0, 32.0, ((0, 8), (1, 32)), jnp.float32),
        "measurement_spread": draw_measurement_spread(jax.random.fold_in(streams_of[4], 71), 0),
    }


def reference(prior_ensemble, measurement_location, measurement_datum, measurement_spread):
    ensemble_size = prior_ensemble.shape[0]
    grid_site_number = prior_ensemble.shape[2]
    norm_factor = math.sqrt(ensemble_size - 1)
    highest = lax.Precision.HIGHEST
    cell_ids = measurement_location.reshape(-1)
    values = measurement_datum.reshape(-1)
    errors = measurement_spread.reshape(-1)
    group_size = OBS_ROWS * 128
    groups = cell_ids.shape[0] // group_size

    def add_group(group_index, totals):
        gram_sum, projected = totals
        first_obs = (group_index * group_size).astype(jnp.int32)
        label_fraction = lax.dynamic_slice_in_dim(cell_ids, first_obs, group_size)
        err_part = lax.dynamic_slice_in_dim(errors, first_obs, group_size)
        val_part = lax.dynamic_slice_in_dim(values, first_obs, group_size)
        picked_lines = prior_ensemble[:, label_fraction // grid_site_number, label_fraction % grid_site_number].astype(jnp.float32)
        mean_obs = lax.optimization_barrier(jnp.mean(picked_lines, axis=0))
        anomaly = (picked_lines - mean_obs).astype(jnp.bfloat16)
        scaled = (anomaly.astype(jnp.float32) / (err_part * norm_factor)).astype(jnp.bfloat16)
        innovation = ((val_part - mean_obs) / err_part).astype(jnp.bfloat16)
        scaled_wide = scaled.astype(jnp.float32)
        gram_sum = gram_sum + lax.dot_general(scaled_wide, scaled_wide, (((1,), (1,)), ((), ())), precision=highest)
        projected = projected + jnp.dot(scaled_wide, innovation.astype(jnp.float32), precision=highest)
        return (gram_sum, projected)
    start_totals = (jnp.zeros((ensemble_size, ensemble_size), jnp.float32), jnp.zeros((ensemble_size,), jnp.float32))
    gram_sum, projected = lax.fori_loop(0, groups, add_group, start_totals)
    identity = jnp.eye(ensemble_size, dtype=jnp.float32)
    system = gram_sum + identity
    norm_scale = jnp.sqrt(jnp.sum(system * system))

    def newton_turn(turn, pair):
        iterate_y, iterate_z = pair
        newton_step = 1.5 * identity - 0.5 * jnp.dot(iterate_z, iterate_y, precision=highest)
        return (jnp.dot(newton_step, iterate_y, precision=highest), jnp.dot(newton_step, iterate_z, precision=highest))
    iterate_y, iterate_z = lax.fori_loop(0, NS_ITERS, newton_turn, (system / norm_scale, identity))
    shift_weights = jnp.dot(iterate_z, projected, precision=highest) / (jnp.sqrt(norm_scale) * norm_factor)
    weights = (iterate_z / jnp.sqrt(norm_scale)).astype(jnp.bfloat16).astype(jnp.float32)
    tile_sequence = grid_site_number // GRID_SHARE_SPAN

    def renew_tile(block_index, analysis):
        initial_grid_site = (block_index * GRID_SHARE_SPAN).astype(jnp.int32)
        tile_fraction = lax.dynamic_slice_in_dim(prior_ensemble, initial_grid_site, GRID_SHARE_SPAN, 2)
        flat_state = tile_fraction.reshape(ensemble_size, 2 * GRID_SHARE_SPAN).astype(jnp.float32)
        mean_state = lax.optimization_barrier(jnp.mean(flat_state, axis=0))
        anomalies = (flat_state - mean_state).astype(jnp.bfloat16).astype(jnp.float32)
        updated = jnp.dot(weights, anomalies, precision=highest)
        mean_shift = jnp.dot(shift_weights, updated, precision=highest)
        block_out = (mean_state + mean_shift + updated).astype(jnp.bfloat16).reshape(ensemble_size, 2, GRID_SHARE_SPAN)
        return lax.dynamic_update_slice_in_dim(analysis, block_out, initial_grid_site, 2)
    return lax.fori_loop(0, tile_sequence, renew_tile, jnp.zeros(prior_ensemble.shape, jnp.bfloat16))
```

```python
import functools
import math

import jax
import jax.numpy as jnp
from jax import lax
from jax.experimental import pallas as pl
from jax.experimental.pallas import tpu as pltpu
from jax.sharding import Mesh
from jax.sharding import PartitionSpec as P

NS_ITERS = 8
MEM = ("mem_0", "mem_1", "mem_2")
CHIPS = ("mem_0", "mem_1", "cell")
F32 = jnp.float32
BF16 = jnp.bfloat16
VMEM = pl.BlockSpec(memory_space=pltpu.VMEM)
SMEM = pl.BlockSpec(memory_space=pltpu.SMEM)
ANY = pl.BlockSpec(memory_space=pl.ANY)


def pack_kernel(x_ref, o_ref, sem):
    blocks, width = o_ref.shape[0], o_ref.shape[3]
    copies = [
        pltpu.make_async_copy(
            x_ref.at[:, :, pl.ds(b * width, width)], o_ref.at[b], sem.at[b]
        )
        for b in range(blocks)
    ]
    for c in copies:
        c.start()
    for c in copies:
        c.wait()


def unpack_kernel(x_ref, o_ref, sem):
    blocks, width = x_ref.shape[0], x_ref.shape[3]
    copies = [
        pltpu.make_async_copy(
            x_ref.at[b], o_ref.at[:, :, pl.ds(b * width, width)], sem.at[b]
        )
        for b in range(blocks)
    ]
    for c in copies:
        c.start()
    for c in copies:
        c.wait()


def rows_of(x_ref, f):
    groups, _, eight, width = x_ref.shape
    return x_ref[:, f].reshape(groups * eight, width)


def contract(a, b, dims):
    return lax.dot_general(a, b, (dims, ((), ())), preferred_element_type=F32)


def gram_kernel(core_ref, slot_ref, datum_ref, spread_ref, x_ref, keep_ref, send_ref, gram_ref):
    groups, fields, eight, width = x_ref.shape
    members = groups * eight
    norm_factor = math.sqrt(members - 1)
    scaled_parts, innovation_parts = [], []
    iota = lax.broadcasted_iota(jnp.int32, (width, 128), 0)
    for r in range(slot_ref.shape[0]):
        slot = slot_ref[r : r + 1, :]
        picked = None
        for f in range(fields):
            chosen = jnp.where(iota == slot - f * width, 1.0, 0.0).astype(BF16)
            term = contract(rows_of(x_ref, f), chosen, ((1,), (0,)))
            picked = term if picked is None else picked + term
        mean = jnp.sum(picked, axis=0, keepdims=True) / members
        anomaly = (picked - mean).astype(BF16).astype(F32)
        error = spread_ref[r : r + 1, :]
        scaled_parts.append((anomaly / (error * norm_factor)).astype(BF16))
        innovation_parts.append(((datum_ref[r : r + 1, :] - mean) / error).astype(BF16))
    scaled = jnp.concatenate(scaled_parts, axis=1)
    innovation = jnp.concatenate(innovation_parts, axis=1).astype(F32)
    innovation = jnp.broadcast_to(innovation, (16, innovation.shape[1])).astype(BF16)
    gram_ref[...] = contract(scaled, scaled, ((1,), (1,)))
    projected = contract(innovation, scaled, ((1,), (1,)))
    for j in range(members // 128):
        gram_ref[members - 8 + j : members - 7 + j, 0:128] = projected[0:1, j * 128 : (j + 1) * 128]
    half = members // 2
    lanes = members // 128
    core = core_ref[0]
    for part, ref in ((core, keep_ref), (1 - core, send_ref)):
        start = pl.multiple_of(part * half, half)
        rows = gram_ref[pl.ds(start, half), :]
        for i in range(half // 8):
            for j in range(lanes):
                ref[i * lanes + j] = rows[i * 8 : i * 8 + 8, j * 128 : j * 128 + 128]


def mean_kernel(x_ref, anomalies_ref, mean_ref):
    groups, fields, eight, width = x_ref.shape
    members = groups * eight
    for f in range(fields):
        x = x_ref[:, f].astype(F32)
        mean = jnp.sum(jnp.sum(x, axis=0), axis=0, keepdims=True) / members
        mean_ref[f : f + 1, :] = mean
        anomalies_ref[:, f] = (x - mean[None]).astype(BF16)


def halves(a):
    high = a.astype(BF16)
    return high, (a - high.astype(F32)).astype(BF16)


def thirds(row):
    high = row.astype(BF16).astype(F32)
    rest = row - high
    middle = rest.astype(BF16).astype(F32)
    low = rest - middle
    pad = jnp.zeros((13, row.shape[1]), F32)
    return jnp.concatenate([high, middle, low, pad], axis=0).astype(BF16)


def times(a, b):
    dims = ((1,), (0,))
    return contract(a[0], b[0], dims) + (contract(a[0], b[1], dims) + contract(a[1], b[0], dims))


def analysis_kernel(core_ref, own_ref, other_ref, anomalies_ref, mean_ref, o_ref, sys_ref, yh, yl, zh, zl, zf):
    members = sys_ref.shape[0]
    norm_factor = math.sqrt(members - 1)
    half, lanes = members // 2, members // 128
    core = core_ref[0]
    for part, ref in ((core, own_ref), (1 - core, other_ref)):
        start = pl.multiple_of(part * half, half)
        for i in range(half // 8):
            for j in range(lanes):
                sys_ref[pl.ds(start + i * 8, 8), j * 128 : (j + 1) * 128] = ref[i * lanes + j]
    tile = sys_ref[members - 8 : members, 0:128]
    projected = jnp.concatenate([tile[j : j + 1, :] for j in range(lanes)], axis=1)
    mirror = jnp.transpose(sys_ref[0:128, members - 128 : members])
    sys_ref[members - 8 : members, 0:128] = mirror[120:128, :]
    row_iota = lax.broadcasted_iota(jnp.int32, (members, members), 0)
    column_iota = lax.broadcasted_iota(jnp.int32, (members, members), 1)
    diagonal = row_iota == column_iota
    system = sys_ref[...] + jnp.where(diagonal, 1.0, 0.0)
    squares = jnp.sum(jnp.sum(system * system, axis=0, keepdims=True), axis=1, keepdims=True)
    norm_scale = jnp.sqrt(squares)
    start_y = system / norm_scale

    def step_of(product):
        return jnp.where(diagonal, 1.5, 0.0) - 0.5 * product

    first = step_of(start_y)
    first_parts = halves(first)
    zh[...], zl[...] = first_parts
    yh[...], yl[...] = halves(times(first_parts, halves(start_y)))

    def turn(_, carry):
        y, z = (yh[...], yl[...]), (zh[...], zl[...])
        step = halves(step_of(times(z, y)))
        yh[...], yl[...] = halves(times(step, y))
        zh[...], zl[...] = halves(times(step, z))
        return carry

    lax.fori_loop(0, NS_ITERS - 2, turn, 0)
    z = (zh[...], zl[...])
    step = halves(step_of(times(z, (yh[...], yl[...]))))
    zf[...] = times(step, z)
    iterate_z = zf[...]
    root = jnp.sqrt(norm_scale)
    dims = ((1,), (0,))
    z = halves(iterate_z)
    three = thirds(projected)
    sent = contract(three, z[0], dims) + contract(three, z[1], dims)
    shift = jnp.sum(sent, axis=0, keepdims=True) / (root * norm_factor)
    weights = (iterate_z / root).astype(BF16)
    combined = jnp.sum(contract(thirds(shift), weights, dims), axis=0, keepdims=True)
    combined = thirds(combined)
    groups, fields, eight, width = anomalies_ref.shape
    for f in range(fields):
        anomalies = rows_of(anomalies_ref, f)
        mean_shift = jnp.sum(contract(combined, anomalies, dims), axis=0, keepdims=True)
        base = mean_ref[f : f + 1, :] + mean_shift
        updated = contract(weights, anomalies, dims)
        o_ref[:, f] = (base + updated).astype(BF16).reshape(groups, eight, width)


def shape(dims, dtype):
    return jax.ShapeDtypeStruct(dims, dtype)


def local(prior_ensemble, measurement_location, measurement_datum, measurement_spread):
    rows, fields, span = prior_ensemble.shape
    peers = lax.axis_size(MEM)
    members = rows * peers
    width = span // peers
    core = lax.axis_index("mem_2").reshape(1).astype(jnp.int32)
    packed = pl.pallas_call(
        pack_kernel,
        out_shape=shape((peers, rows, fields, width), BF16),
        in_specs=[ANY],
        out_specs=ANY,
        scratch_shapes=[pltpu.SemaphoreType.DMA((peers,))],
        name="pack",
    )(prior_ensemble)
    gathered = lax.all_to_all(packed.reshape(members, fields, width), MEM, 0, 0, tiled=True)
    groups = members // 8
    state = gathered.reshape(groups, 8, fields, width).transpose(0, 2, 1, 3)
    sites = span * lax.axis_size("cell")
    block_start = (lax.axis_index("cell") * peers + lax.axis_index(MEM)) * width
    slots = measurement_location // sites * width + (measurement_location % sites - block_start)
    chips = lax.axis_size(CHIPS)
    tiles = shape((chips, 8, 128), F32)
    keep, send = pl.pallas_call(
        gram_kernel,
        out_shape=(tiles, tiles),
        in_specs=[SMEM, VMEM, VMEM, VMEM, VMEM],
        out_specs=(VMEM, VMEM),
        scratch_shapes=[pltpu.VMEM((members, members), F32)],
        name="gram",
    )(core, slots, measurement_datum, measurement_spread, state)
    swap = [(0, 1), (1, 0)]
    part = keep + lax.ppermute(send, "mem_2", swap)
    part = lax.all_to_all(part, CHIPS, 0, 0, tiled=True)
    total = jnp.broadcast_to(jnp.sum(part, axis=0, keepdims=True), part.shape)
    own = lax.all_to_all(total, CHIPS, 0, 0, tiled=True)
    other = lax.ppermute(own, "mem_2", swap)
    anomalies, mean = pl.pallas_call(
        mean_kernel,
        out_shape=(shape(state.shape, BF16), shape((fields, width), F32)),
        in_specs=[VMEM],
        out_specs=(VMEM, VMEM),
        name="mean",
    )(state)
    square = pltpu.VMEM((members, members), BF16)
    whole = pltpu.VMEM((members, members), F32)
    analysis = pl.pallas_call(
        analysis_kernel,
        out_shape=shape(state.shape, BF16),
        in_specs=[SMEM, VMEM, VMEM, VMEM, VMEM],
        out_specs=VMEM,
        scratch_shapes=[whole, square, square, square, square, whole],
        name="analysis",
    )(core, own, other, anomalies, mean)
    analysis = analysis.transpose(0, 2, 1, 3).reshape(members, fields, width)
    returned = lax.all_to_all(analysis, MEM, 0, 0, tiled=True)
    return pl.pallas_call(
        unpack_kernel,
        out_shape=shape(prior_ensemble.shape, BF16),
        in_specs=[ANY],
        out_specs=ANY,
        scratch_shapes=[pltpu.SemaphoreType.DMA((peers,))],
        name="unpack",
    )(returned.reshape(peers, rows, fields, width))


def solution(mesh):
    torus = Mesh(
        mesh.devices.reshape(4, 4, 2, mesh.shape["cell"]), ("mem_0", "mem_1", "mem_2", "cell")
    )
    in_specs = (P(MEM, None, "cell"), P("cell", MEM), P("cell", MEM), P("cell", MEM))
    out_specs = P(MEM, None, "cell")
    return jax.shard_map(local, mesh=torus, in_specs=in_specs, out_specs=out_specs, check_vma=False)
```

```python
import math

import jax
import jax.numpy as jnp
from jax import lax
from jax.experimental import pallas as pl
from jax.experimental.pallas import tpu as pltpu
from jax.sharding import Mesh
from jax.sharding import PartitionSpec as P

NS_ITERS = 8
MEM = ("mem_0", "mem_1", "mem_2")
PLANE = ("mem_0", "mem_1")
F32 = jnp.float32
BF16 = jnp.bfloat16
VMEM = pl.BlockSpec(memory_space=pltpu.VMEM)
SMEM = pl.BlockSpec(memory_space=pltpu.SMEM)


def tiles_of(members):
    blocks = members // 128
    return [
        (row * 128 + i * 8, column * 128)
        for row in range(blocks)
        for column in range(row, blocks)
        for i in range(16)
    ]


def rows_of(x_ref, f):
    groups, _, rows, width = x_ref.shape
    return x_ref[:, f].reshape(groups * rows, width)


def contract(a, b, dims):
    return lax.dot_general(a, b, (dims, ((), ())), preferred_element_type=F32)


def gram_kernel(core_ref, slot_ref, datum_ref, spread_ref, x_ref, keep_ref, send_ref, sum_ref):
    groups, fields, rows, width = x_ref.shape
    members = groups * rows
    norm_factor = math.sqrt(members - 1)
    scaled_parts, innovation_parts = [], []
    iota = lax.broadcasted_iota(jnp.int32, (width, 256), 0)

    def pair(ref, r):
        return jnp.concatenate([ref[r : r + 1, :], ref[r + 1 : r + 2, :]], axis=1)

    for r in range(0, slot_ref.shape[0], 2):
        slot = pair(slot_ref, r)
        picked = None
        for f in range(fields):
            chosen = jnp.where(iota == slot - f * width, 1.0, 0.0).astype(BF16)
            term = contract(rows_of(x_ref, f), chosen, ((1,), (0,)))
            picked = term if picked is None else picked + term
        mean = jnp.sum(picked, axis=0, keepdims=True) / members
        anomaly = (picked - mean).astype(BF16).astype(F32)
        error = pair(spread_ref, r)
        scaled_parts.append((anomaly / (error * norm_factor)).astype(BF16))
        innovation_parts.append(((pair(datum_ref, r) - mean) / error).astype(BF16))
    scaled = jnp.concatenate(scaled_parts, axis=1)
    innovation = jnp.concatenate(innovation_parts, axis=1).astype(F32)
    innovation = jnp.broadcast_to(innovation, (16, innovation.shape[1])).astype(BF16)
    gram = contract(scaled, scaled, ((1,), (1,)))
    projected = contract(innovation, scaled, ((1,), (1,)))
    tiles = tiles_of(members)
    for t, (row, column) in enumerate(tiles):
        sum_ref[t] = gram[row : row + 8, column : column + 128]
    sum_ref[len(tiles) :] = jnp.zeros_like(sum_ref[len(tiles) :])
    for j in range(members // 128):
        sum_ref[len(tiles), j : j + 1, :] = projected[0:1, j * 128 : (j + 1) * 128]
    core = core_ref[0]
    half = keep_ref.shape[0]
    keep_ref[...] = sum_ref[pl.ds(core * half, half)]
    send_ref[...] = sum_ref[pl.ds((1 - core) * half, half)]


def mean_kernel(x_ref, anomalies_ref, mean_ref):
    groups, fields, rows, width = x_ref.shape
    members = groups * rows
    for f in range(fields):
        x = x_ref[:, f].astype(F32)
        mean = jnp.sum(jnp.sum(x, axis=0), axis=0, keepdims=True) / members
        mean_ref[f : f + 1, :] = mean
        anomalies_ref[:, f] = (x - mean[None]).astype(BF16)


def halves(a):
    high = a.astype(BF16)
    return high, (a - high.astype(F32)).astype(BF16)


def thirds(row):
    high = row.astype(BF16).astype(F32)
    rest = row - high
    middle = rest.astype(BF16).astype(F32)
    low = rest - middle
    pad = jnp.zeros((13, row.shape[1]), F32)
    return jnp.concatenate([high, middle, low, pad], axis=0).astype(BF16)


def times(a, b):
    dims = ((1,), (0,))
    return contract(a[0], b[0], dims) + (contract(a[0], b[1], dims) + contract(a[1], b[0], dims))


def analysis_kernel(
    core_ref, own_ref, other_ref, anomalies_ref, mean_ref, o_ref, sum_ref, sys_ref, yh, yl, zh, zl, zf
):
    members = sys_ref.shape[0]
    norm_factor = math.sqrt(members - 1)
    blocks = members // 128
    core = core_ref[0]
    half = own_ref.shape[0]
    sum_ref[pl.ds(core * half, half)] = own_ref[...]
    sum_ref[pl.ds((1 - core) * half, half)] = other_ref[...]
    tiles = tiles_of(members)
    for t, (row, column) in enumerate(tiles):
        sys_ref[row : row + 8, column : column + 128] = sum_ref[t]
    for i in range(blocks):
        for j in range(i + 1, blocks):
            upper = sys_ref[i * 128 : i * 128 + 128, j * 128 : j * 128 + 128]
            sys_ref[j * 128 : j * 128 + 128, i * 128 : i * 128 + 128] = jnp.transpose(upper)
    projected = jnp.concatenate([sum_ref[len(tiles), j : j + 1, :] for j in range(blocks)], axis=1)
    row_iota = lax.broadcasted_iota(jnp.int32, (members, members), 0)
    column_iota = lax.broadcasted_iota(jnp.int32, (members, members), 1)
    diagonal = row_iota == column_iota
    system = sys_ref[...] + jnp.where(diagonal, 1.0, 0.0)
    squares = jnp.sum(jnp.sum(system * system, axis=0, keepdims=True), axis=1, keepdims=True)
    norm_scale = jnp.sqrt(squares)
    start_y = system / norm_scale

    def step_of(product):
        return jnp.where(diagonal, 1.5, 0.0) - 0.5 * product

    first = step_of(start_y)
    first_parts = halves(first)
    zh[...], zl[...] = first_parts
    yh[...], yl[...] = halves(times(first_parts, halves(start_y)))

    def turn(_, carry):
        y, z = (yh[...], yl[...]), (zh[...], zl[...])
        step = halves(step_of(times(z, y)))
        yh[...], yl[...] = halves(times(step, y))
        zh[...], zl[...] = halves(times(step, z))
        return carry

    lax.fori_loop(0, NS_ITERS - 2, turn, 0)
    z = (zh[...], zl[...])
    step = halves(step_of(times(z, (yh[...], yl[...]))))
    zf[...] = times(step, z)
    iterate_z = zf[...]
    root = jnp.sqrt(norm_scale)
    dims = ((1,), (0,))
    z = halves(iterate_z)
    three = thirds(projected)
    sent = contract(three, z[0], dims) + contract(three, z[1], dims)
    shift = jnp.sum(sent, axis=0, keepdims=True) / (root * norm_factor)
    weights = (iterate_z / root).astype(BF16)
    combined = jnp.sum(contract(thirds(shift), weights, dims), axis=0, keepdims=True)
    combined = thirds(combined)
    groups, fields, rows, width = anomalies_ref.shape
    for f in range(fields):
        anomalies = rows_of(anomalies_ref, f)
        mean_shift = jnp.sum(contract(combined, anomalies, dims), axis=0, keepdims=True)
        base = mean_ref[f : f + 1, :] + mean_shift
        updated = contract(weights, anomalies, dims)
        o_ref[:, f] = (base + updated).astype(BF16).reshape(groups, rows, width)


def shape(dims, dtype):
    return jax.ShapeDtypeStruct(dims, dtype)


def total_for(part, sources, targets):
    total = jnp.sum(part.reshape(sources, -1, *part.shape[1:]), axis=0)
    copies = jnp.broadcast_to(total[None], (targets, *total.shape))
    return copies.reshape(-1, *total.shape[1:])


def local(prior_ensemble, measurement_location, measurement_datum, measurement_spread):
    rows, fields, span = prior_ensemble.shape
    peers = lax.axis_size(MEM)
    members = rows * peers
    width = span // peers
    core = lax.axis_index("mem_2").reshape(1).astype(jnp.int32)
    state = prior_ensemble.reshape(rows, fields, peers, width).transpose(2, 1, 0, 3)
    state = lax.all_to_all(state, MEM, 0, 0, tiled=True)
    sites = span * lax.axis_size("cell")
    block_start = (lax.axis_index("cell") * peers + lax.axis_index(MEM)) * width
    slots = measurement_location // sites * width + (measurement_location % sites - block_start)
    plane, planes = lax.axis_size(PLANE), lax.axis_size("cell")
    share = -(-(len(tiles_of(members)) + 1) // (2 * plane))
    half = shape((share * plane, 8, 128), F32)
    both = pltpu.VMEM((2 * share * plane, 8, 128), F32)
    keep, send = pl.pallas_call(
        gram_kernel,
        out_shape=(half, half),
        in_specs=[SMEM, VMEM, VMEM, VMEM, VMEM],
        out_specs=(VMEM, VMEM),
        scratch_shapes=[both],
        name="gram",
    )(core, slots, measurement_datum, measurement_spread, state)
    swap = [(0, 1), (1, 0)]
    part = keep + lax.ppermute(send, "mem_2", swap)
    part = lax.all_to_all(part, PLANE, 0, 0, tiled=True)
    part = total_for(part, plane, planes)
    part = lax.all_to_all(part, "cell", 0, 0, tiled=True)
    part = total_for(part, planes, plane)
    own = lax.all_to_all(part, PLANE, 0, 0, tiled=True)
    other = lax.ppermute(own, "mem_2", swap)
    anomalies, mean = pl.pallas_call(
        mean_kernel,
        out_shape=(shape(state.shape, BF16), shape((fields, width), F32)),
        in_specs=[VMEM],
        out_specs=(VMEM, VMEM),
        name="mean",
    )(state)
    square = pltpu.VMEM((members, members), BF16)
    whole = pltpu.VMEM((members, members), F32)
    analysis = pl.pallas_call(
        analysis_kernel,
        out_shape=shape(state.shape, BF16),
        in_specs=[SMEM, VMEM, VMEM, VMEM, VMEM],
        out_specs=VMEM,
        scratch_shapes=[both, whole, square, square, square, square, whole],
        name="analysis",
    )(core, own, other, anomalies, mean)
    returned = lax.all_to_all(analysis, MEM, 0, 0, tiled=True)
    return returned.transpose(2, 1, 0, 3).reshape(rows, fields, span)


def solution(mesh):
    torus = Mesh(
        mesh.devices.reshape(4, 4, 2, mesh.shape["cell"]), ("mem_0", "mem_1", "mem_2", "cell")
    )
    in_specs = (P(MEM, None, "cell"), P("cell", MEM), P("cell", MEM), P("cell", MEM))
    out_specs = P(MEM, None, "cell")
    return jax.shard_map(local, mesh=torus, in_specs=in_specs, out_specs=out_specs, check_vma=False)
```

```python
import math

import jax
import jax.numpy as jnp
from jax import lax
from jax.experimental import pallas as pl
from jax.experimental.pallas import tpu as pltpu
from jax.sharding import Mesh
from jax.sharding import PartitionSpec as P

NS_ITERS = 8
MEM = ("mem_0", "mem_1", "mem_2")
PLANE = ("mem_0", "mem_1")
F32 = jnp.float32
BF16 = jnp.bfloat16
VMEM = pl.BlockSpec(memory_space=pltpu.VMEM)
HBM = pl.BlockSpec(memory_space=pltpu.HBM)
SMEM = pl.BlockSpec(memory_space=pltpu.SMEM)


def pack_kernel(x_ref, o_ref, buffer, sem, packed, sent):
    parts, width = buffer.shape[0], o_ref.shape[3]
    span = buffer.shape[3]
    each = span // width
    copies = [
        pltpu.make_async_copy(x_ref.at[:, :, pl.ds(i * span, span)], buffer.at[i], sem.at[i])
        for i in range(parts)
    ]
    for c in copies:
        c.start()
    results = [
        pltpu.make_async_copy(
            packed.at[pl.ds(i * each, each)], o_ref.at[pl.ds(i * each, each)], sent.at[i]
        )
        for i in range(parts)
    ]
    for i in range(parts):
        copies[i].wait()
        for k in range(each):
            block = buffer[i, :, :, k * width : (k + 1) * width]
            packed[i * each + k] = jnp.transpose(block, (1, 0, 2))
        results[i].start()
    for c in results:
        c.wait()


def unpack_kernel(y_ref, o_ref, buffer, sem):
    parts, width = buffer.shape[0], y_ref.shape[3]
    span = buffer.shape[3]
    each = span // width
    copies = []
    for i in range(parts):
        for k in range(each):
            block = jnp.transpose(y_ref[i * each + k], (1, 0, 2))
            buffer[i, :, :, k * width : (k + 1) * width] = block
        copy = pltpu.make_async_copy(
            buffer.at[i], o_ref.at[:, :, pl.ds(i * span, span)], sem.at[i]
        )
        copy.start()
        copies.append(copy)
    for c in copies:
        c.wait()


def tiles_of(members):
    blocks = members // 128
    return [
        (row * 128 + i * 8, column * 128)
        for row in range(blocks)
        for column in range(row, blocks)
        for i in range(16)
    ]


def rows_of(x_ref, f):
    groups, _, rows, width = x_ref.shape
    return x_ref[:, f].reshape(groups * rows, width)


def contract(a, b, dims):
    return lax.dot_general(a, b, (dims, ((), ())), preferred_element_type=F32)


def gram_kernel(core_ref, slot_ref, datum_ref, spread_ref, x_ref, keep_ref, send_ref, sum_ref):
    groups, fields, rows, width = x_ref.shape
    members = groups * rows
    norm_factor = math.sqrt(members - 1)
    scaled_parts, innovation_parts = [], []
    iota = lax.broadcasted_iota(jnp.int32, (width, 256), 0)

    def pair(ref, r):
        return jnp.concatenate([ref[r : r + 1, :], ref[r + 1 : r + 2, :]], axis=1)

    for r in range(0, slot_ref.shape[0], 2):
        slot = pair(slot_ref, r)
        picked = None
        for f in range(fields):
            chosen = jnp.where(iota == slot - f * width, 1.0, 0.0).astype(BF16)
            term = contract(rows_of(x_ref, f), chosen, ((1,), (0,)))
            picked = term if picked is None else picked + term
        mean = jnp.sum(picked, axis=0, keepdims=True) / members
        anomaly = (picked - mean).astype(BF16).astype(F32)
        error = pair(spread_ref, r)
        scaled_parts.append((anomaly / (error * norm_factor)).astype(BF16))
        innovation_parts.append(((pair(datum_ref, r) - mean) / error).astype(BF16))
    scaled = jnp.concatenate(scaled_parts, axis=1)
    innovation = jnp.concatenate(innovation_parts, axis=1).astype(F32)
    innovation = jnp.broadcast_to(innovation, (16, innovation.shape[1])).astype(BF16)
    gram = contract(scaled, scaled, ((1,), (1,)))
    projected = contract(innovation, scaled, ((1,), (1,)))
    tiles = tiles_of(members)
    for t, (row, column) in enumerate(tiles):
        sum_ref[t] = gram[row : row + 8, column : column + 128]
    sum_ref[len(tiles) :] = jnp.zeros_like(sum_ref[len(tiles) :])
    for j in range(members // 128):
        sum_ref[len(tiles), j : j + 1, :] = projected[0:1, j * 128 : (j + 1) * 128]
    core = core_ref[0]
    half = keep_ref.shape[0]
    keep_ref[...] = sum_ref[pl.ds(core * half, half)]
    send_ref[...] = sum_ref[pl.ds((1 - core) * half, half)]


def mean_kernel(x_ref, anomalies_ref, mean_ref):
    groups, fields, rows, width = x_ref.shape
    members = groups * rows
    for f in range(fields):
        x = x_ref[:, f].astype(F32)
        mean = jnp.sum(jnp.sum(x, axis=0), axis=0, keepdims=True) / members
        mean_ref[f : f + 1, :] = mean
        anomalies_ref[:, f] = (x - mean[None]).astype(BF16)


def halves(a):
    high = a.astype(BF16)
    return high, (a - high.astype(F32)).astype(BF16)


def thirds(row):
    high = row.astype(BF16).astype(F32)
    rest = row - high
    middle = rest.astype(BF16).astype(F32)
    low = rest - middle
    pad = jnp.zeros((13, row.shape[1]), F32)
    return jnp.concatenate([high, middle, low, pad], axis=0).astype(BF16)


def product(a, b):
    size = a[0].shape[0]
    half = size // 2
    dims = ((1,), (0,))

    def block(r, c):
        ah, al = (m[r : r + half, :] for m in a)
        bh, bl = (m[:, c : c + half] for m in b)
        return contract(ah, bh, dims) + (contract(ah, bl, dims) + contract(al, bh, dims))

    return block(0, 0), block(0, half), block(half, half)


def keep_product(pair, blocks):
    high_ref, low_ref = pair
    half = high_ref.shape[0] // 2
    first, side, last = blocks
    places = ((0, 0, first), (0, half, side), (half, half, last), (half, 0, jnp.transpose(side)))
    for r, c, value in places:
        high, low = halves(value)
        high_ref[r : r + half, c : c + half] = high
        low_ref[r : r + half, c : c + half] = low


def analysis_kernel(
    core_ref,
    own_ref,
    other_ref,
    source_ref,
    mean_ref,
    o_ref,
    anomalies_ref,
    sem,
    sum_ref,
    sys_ref,
    yh,
    yl,
    zh,
    zl,
    th,
    tl,
):
    load = pltpu.make_async_copy(source_ref, anomalies_ref, sem)
    load.start()
    members = sys_ref.shape[0]
    norm_factor = math.sqrt(members - 1)
    blocks = members // 128
    core = core_ref[0]
    half = own_ref.shape[0]
    sum_ref[pl.ds(core * half, half)] = own_ref[...]
    sum_ref[pl.ds((1 - core) * half, half)] = other_ref[...]
    tiles = tiles_of(members)
    for t, (row, column) in enumerate(tiles):
        sys_ref[row : row + 8, column : column + 128] = sum_ref[t]
    for i in range(blocks):
        for j in range(i + 1, blocks):
            upper = sys_ref[i * 128 : i * 128 + 128, j * 128 : j * 128 + 128]
            sys_ref[j * 128 : j * 128 + 128, i * 128 : i * 128 + 128] = jnp.transpose(upper)
    projected = jnp.concatenate([sum_ref[len(tiles), j : j + 1, :] for j in range(blocks)], axis=1)
    row_iota = lax.broadcasted_iota(jnp.int32, (members, members), 0)
    column_iota = lax.broadcasted_iota(jnp.int32, (members, members), 1)
    diagonal = row_iota == column_iota
    system = sys_ref[...] + jnp.where(diagonal, 1.0, 0.0)
    squares = jnp.sum(jnp.sum(system * system, axis=0, keepdims=True), axis=1, keepdims=True)
    norm_scale = jnp.sqrt(squares)
    start_y = system / norm_scale

    half_size = members // 2
    half_diagonal = diagonal[:half_size, :half_size]
    y, z, t = (yh, yl), (zh, zl), (th, tl)

    def step_of(blocks):
        first, side, last = blocks
        whole = jnp.where(half_diagonal, 1.5, 0.0)
        return whole - 0.5 * first, -0.5 * side, whole - 0.5 * last

    zh[...], zl[...] = halves(jnp.where(diagonal, 1.5, 0.0) - 0.5 * start_y)
    th[...], tl[...] = halves(start_y)
    keep_product(y, product(z, t))

    def turn(_, carry):
        keep_product(t, step_of(product(z, y)))
        next_y, next_z = product(t, y), product(t, z)
        keep_product(y, next_y)
        keep_product(z, next_z)
        return carry

    lax.fori_loop(0, NS_ITERS - 2, turn, 0)
    keep_product(t, step_of(product(z, y)))
    first, side, last = product(t, z)
    sys_ref[:half_size, :half_size] = first
    sys_ref[:half_size, half_size:] = side
    sys_ref[half_size:, half_size:] = last
    sys_ref[half_size:, :half_size] = jnp.transpose(side)
    iterate_z = sys_ref[...]
    root = jnp.sqrt(norm_scale)
    dims = ((1,), (0,))
    zs = halves(iterate_z)
    three = thirds(projected)
    sent = contract(three, zs[0], dims) + contract(three, zs[1], dims)
    shift = jnp.sum(sent, axis=0, keepdims=True) / (root * norm_factor)
    weights = (iterate_z / root).astype(BF16)
    combined = jnp.sum(contract(thirds(shift), weights, dims), axis=0, keepdims=True)
    combined = thirds(combined)
    groups, fields, rows, width = anomalies_ref.shape
    load.wait()
    for f in range(fields):
        anomalies = rows_of(anomalies_ref, f)
        mean_shift = jnp.sum(contract(combined, anomalies, dims), axis=0, keepdims=True)
        base = mean_ref[f : f + 1, :] + mean_shift
        updated = contract(weights, anomalies, dims)
        o_ref[:, f] = (base + updated).astype(BF16).reshape(groups, rows, width)


def far(a):
    return pltpu.with_memory_space_constraint(a, pltpu.HBM)


def near(a):
    return pltpu.with_memory_space_constraint(a, pltpu.VMEM)


def total_for(part, sources, targets):
    total = jnp.sum(part.reshape(sources, -1, *part.shape[1:]), axis=0)
    copies = jnp.broadcast_to(total[None], (targets, *total.shape))
    return copies.reshape(-1, *total.shape[1:])


def local(prior_ensemble, measurement_location, measurement_datum, measurement_spread):
    rows, fields, span = prior_ensemble.shape
    peers = lax.axis_size(MEM)
    members = rows * peers
    width = span // peers
    core = lax.axis_index("mem_2").reshape(1).astype(jnp.int32)
    parts = 4
    staging = [pltpu.VMEM((parts, rows, fields, span // parts), BF16), pltpu.SemaphoreType.DMA((parts,))]
    tiled = pltpu.VMEM((peers, fields, rows, width), BF16)
    packed = pl.pallas_call(
        pack_kernel,
        out_shape=pltpu.HBM(tiled.shape, BF16),
        in_specs=[HBM],
        out_specs=HBM,
        scratch_shapes=staging + [tiled, pltpu.SemaphoreType.DMA((parts,))],
        compiler_params=pltpu.CompilerParams(vmem_limit_bytes=8 << 20),
        name="pack",
    )(far(prior_ensemble))
    state = near(lax.all_to_all(packed, MEM, 0, 0, tiled=True))
    sites = span * lax.axis_size("cell")
    block_start = (lax.axis_index("cell") * peers + lax.axis_index(MEM)) * width
    slots = measurement_location // sites * width + (measurement_location % sites - block_start)
    plane, planes = lax.axis_size(PLANE), lax.axis_size("cell")
    share = -(-(len(tiles_of(members)) + 1) // (2 * plane))
    half = pltpu.VMEM((share * plane, 8, 128), F32)
    both = pltpu.VMEM((2 * share * plane, 8, 128), F32)
    keep, send = pl.pallas_call(
        gram_kernel,
        out_shape=(half, half),
        in_specs=[SMEM, VMEM, VMEM, VMEM, VMEM],
        out_specs=(VMEM, VMEM),
        scratch_shapes=[both],
        compiler_params=pltpu.CompilerParams(vmem_limit_bytes=24 << 20),
        name="gram",
    )(core, slots, measurement_datum, measurement_spread, state)
    swap = [(0, 1), (1, 0)]
    part = keep + lax.ppermute(send, "mem_2", swap)
    part = lax.all_to_all(part, PLANE, 0, 0, tiled=True)
    part = total_for(part, plane, planes)
    part = lax.all_to_all(part, "cell", 0, 0, tiled=True)
    anomalies, mean = pl.pallas_call(
        mean_kernel,
        out_shape=(pltpu.HBM(tiled.shape, BF16), pltpu.VMEM((fields, width), F32)),
        in_specs=[VMEM],
        out_specs=(VMEM, VMEM),
        compiler_params=pltpu.CompilerParams(vmem_limit_bytes=24 << 20),
        name="mean",
    )(state)
    part, anomalies, mean = lax.optimization_barrier((part, anomalies, mean))
    part = total_for(part, planes, plane)
    own = lax.all_to_all(part, PLANE, 0, 0, tiled=True)
    other = lax.ppermute(own, "mem_2", swap)
    square = pltpu.VMEM((members, members), BF16)
    whole = pltpu.VMEM((members, members), F32)
    analysis = pl.pallas_call(
        analysis_kernel,
        out_shape=tiled,
        in_specs=[SMEM, VMEM, VMEM, HBM, VMEM],
        out_specs=VMEM,
        scratch_shapes=[tiled, pltpu.SemaphoreType.DMA, both, whole] + [square] * 6,
        compiler_params=pltpu.CompilerParams(vmem_limit_bytes=32 << 20),
        name="analysis",
    )(core, near(own), near(other), far(anomalies), near(mean))
    returned = lax.all_to_all(analysis, MEM, 0, 0, tiled=True)
    return pl.pallas_call(
        unpack_kernel,
        out_shape=jax.ShapeDtypeStruct(prior_ensemble.shape, BF16),
        in_specs=[VMEM],
        out_specs=HBM,
        scratch_shapes=staging,
        compiler_params=pltpu.CompilerParams(vmem_limit_bytes=8 << 20),
        name="unpack",
    )(near(returned))


def solution(mesh):
    torus = Mesh(
        mesh.devices.reshape(4, 4, 2, mesh.shape["cell"]), ("mem_0", "mem_1", "mem_2", "cell")
    )
    in_specs = (P(MEM, None, "cell"), P("cell", MEM), P("cell", MEM), P("cell", MEM))
    out_specs = P(MEM, None, "cell")
    return jax.shard_map(local, mesh=torus, in_specs=in_specs, out_specs=out_specs, check_vma=False)
```

```python
import functools
import math

import jax
import jax.numpy as jnp
from jax import lax
from jax.experimental import pallas as pl
from jax.experimental.pallas import tpu as pltpu
from jax.sharding import Mesh
from jax.sharding import PartitionSpec as P

NS_ITERS = 8
MEM = ("mem_0", "mem_1", "mem_2")
PLANE = ("mem_0", "mem_1")
F32 = jnp.float32
BF16 = jnp.bfloat16
VMEM = pl.BlockSpec(memory_space=pltpu.VMEM)
HBM = pl.BlockSpec(memory_space=pltpu.HBM)
SMEM = pl.BlockSpec(memory_space=pltpu.SMEM)


def pack_kernel(x_ref, o_ref, buffer, sem, packed, sent):
    parts, width = buffer.shape[0], o_ref.shape[3]
    span = buffer.shape[3]
    each = span // width
    copies = [
        pltpu.make_async_copy(x_ref.at[:, :, pl.ds(i * span, span)], buffer.at[i], sem.at[i])
        for i in range(parts)
    ]
    for c in copies:
        c.start()
    results = [
        pltpu.make_async_copy(
            packed.at[pl.ds(i * each, each)], o_ref.at[pl.ds(i * each, each)], sent.at[i]
        )
        for i in range(parts)
    ]
    for i in range(parts):
        copies[i].wait()
        for k in range(each):
            block = buffer[i, :, :, k * width : (k + 1) * width]
            packed[i * each + k] = jnp.transpose(block, (1, 0, 2))
        results[i].start()
    for c in results:
        c.wait()


def unpack_kernel(y_ref, o_ref, buffer, sem):
    parts, width = buffer.shape[0], y_ref.shape[3]
    span = buffer.shape[3]
    each = span // width
    copies = []
    for i in range(parts):
        for k in range(each):
            block = jnp.transpose(y_ref[i * each + k], (1, 0, 2))
            buffer[i, :, :, k * width : (k + 1) * width] = block
        copy = pltpu.make_async_copy(
            buffer.at[i], o_ref.at[:, :, pl.ds(i * span, span)], sem.at[i]
        )
        copy.start()
        copies.append(copy)
    for c in copies:
        c.wait()


def tiles_of(members):
    blocks = members // 128
    return [
        (row * 128 + i * 8, column * 128)
        for row in range(blocks)
        for column in range(row, blocks)
        for i in range(16)
    ]


def rows_of(x_ref, f):
    groups, _, rows, width = x_ref.shape
    return x_ref[:, f].reshape(groups * rows, width)


def contract(a, b, dims):
    return lax.dot_general(a, b, (dims, ((), ())), preferred_element_type=F32)


def gram_kernel(
    core_ref, start_ref, location_ref, datum_ref, spread_ref, x_ref, keep_ref, send_ref, sum_ref, *, sites
):
    groups, fields, rows, width = x_ref.shape
    members = groups * rows
    norm_factor = math.sqrt(members - 1)
    scaled_parts, innovation_parts = [], []
    iota = lax.broadcasted_iota(jnp.int32, (width, 256), 0)

    def pair(ref, r):
        return jnp.concatenate([ref[r : r + 1, :], ref[r + 1 : r + 2, :]], axis=1)

    start = start_ref[0]
    for r in range(0, location_ref.shape[0], 2):
        location = pair(location_ref, r)
        picked = None
        for f in range(fields):
            chosen = jnp.where(iota == location - (start + f * sites), 1.0, 0.0).astype(BF16)
            term = contract(rows_of(x_ref, f), chosen, ((1,), (0,)))
            picked = term if picked is None else picked + term
        mean = jnp.sum(picked, axis=0, keepdims=True) / members
        anomaly = (picked - mean).astype(BF16).astype(F32)
        error = pair(spread_ref, r)
        scaled_parts.append((anomaly / (error * norm_factor)).astype(BF16))
        innovation_parts.append(((pair(datum_ref, r) - mean) / error).astype(BF16))
    scaled = jnp.concatenate(scaled_parts, axis=1)
    innovation = jnp.concatenate(innovation_parts, axis=1).astype(F32)
    innovation = jnp.broadcast_to(innovation, (16, innovation.shape[1])).astype(BF16)
    gram = contract(scaled, scaled, ((1,), (1,)))
    projected = contract(innovation, scaled, ((1,), (1,)))
    tiles = tiles_of(members)
    for t, (row, column) in enumerate(tiles):
        sum_ref[t] = gram[row : row + 8, column : column + 128]
    rows = jnp.concatenate(
        [projected[0:1, j * 128 : (j + 1) * 128] for j in range(members // 128)], axis=0
    )
    rows = jnp.concatenate([rows, pltpu.roll(rows, 64, 1)], axis=0)
    low_lanes = lax.broadcasted_iota(jnp.int32, rows.shape, 1) < 64
    sum_ref[len(tiles) - 1] = jnp.where(low_lanes, rows, sum_ref[len(tiles) - 1])
    core = core_ref[0]
    half = keep_ref.shape[0]
    keep_ref[...] = sum_ref[pl.ds(core * half, half)]
    send_ref[...] = sum_ref[pl.ds((1 - core) * half, half)]


def mean_kernel(x_ref, anomalies_ref, mean_ref):
    groups, fields, rows, width = x_ref.shape
    members = groups * rows
    for f in range(fields):
        x = x_ref[:, f].astype(F32)
        mean = jnp.sum(jnp.sum(x, axis=0), axis=0, keepdims=True) / members
        mean_ref[f : f + 1, :] = mean
        anomalies_ref[:, f] = (x - mean[None]).astype(BF16)


def halves(a):
    high = a.astype(BF16)
    return high, (a - high.astype(F32)).astype(BF16)


def thirds(row):
    high = row.astype(BF16).astype(F32)
    rest = row - high
    middle = rest.astype(BF16).astype(F32)
    low = rest - middle
    pad = jnp.zeros((13, row.shape[1]), F32)
    return jnp.concatenate([high, middle, low, pad], axis=0).astype(BF16)


def product(a, b):
    size = a[0].shape[0]
    half = size // 2
    dims = ((1,), (0,))

    def block(r, c):
        ah, al = (m[r : r + half, :] for m in a)
        bh, bl = (m[:, c : c + half] for m in b)
        return contract(ah, bh, dims) + (contract(ah, bl, dims) + contract(al, bh, dims))

    return block(0, 0), block(0, half), block(half, half)


def keep_product(pair, blocks):
    high_ref, low_ref = pair
    half = high_ref.shape[0] // 2
    first, side, last = blocks
    places = ((0, 0, first), (0, half, side), (half, half, last), (half, 0, jnp.transpose(side)))
    for r, c, value in places:
        high, low = halves(value)
        high_ref[r : r + half, c : c + half] = high
        low_ref[r : r + half, c : c + half] = low


def analysis_kernel(
    core_ref,
    own_ref,
    other_ref,
    source_ref,
    mean_ref,
    o_ref,
    anomalies_ref,
    sem,
    sum_ref,
    sys_ref,
    yh,
    yl,
    zh,
    zl,
    th,
    tl,
):
    load = pltpu.make_async_copy(source_ref, anomalies_ref, sem)
    load.start()
    members = sys_ref.shape[0]
    norm_factor = math.sqrt(members - 1)
    blocks = members // 128
    core = core_ref[0]
    half = own_ref.shape[0]
    sum_ref[pl.ds(core * half, half)] = own_ref[...]
    sum_ref[pl.ds((1 - core) * half, half)] = other_ref[...]
    tiles = tiles_of(members)
    for t, (row, column) in enumerate(tiles):
        sys_ref[row : row + 8, column : column + 128] = sum_ref[t]
    for i in range(blocks):
        for j in range(i + 1, blocks):
            upper = sys_ref[i * 128 : i * 128 + 128, j * 128 : j * 128 + 128]
            sys_ref[j * 128 : j * 128 + 128, i * 128 : i * 128 + 128] = jnp.transpose(upper)
    tile = sum_ref[len(tiles) - 1]
    low_lanes = lax.broadcasted_iota(jnp.int32, (blocks, 128), 1) < 64
    projected = jnp.where(low_lanes, tile[0:blocks], pltpu.roll(tile[blocks : 2 * blocks], 64, 1))
    projected = jnp.concatenate([projected[j : j + 1, :] for j in range(blocks)], axis=1)
    corner = sys_ref[members - 128 :, members - 128 :]
    low_lanes = lax.broadcasted_iota(jnp.int32, tile.shape, 1) < 64
    sys_ref[members - 8 :, members - 128 :] = jnp.where(low_lanes, jnp.transpose(corner)[120:128], tile)
    row_iota = lax.broadcasted_iota(jnp.int32, (members, members), 0)
    column_iota = lax.broadcasted_iota(jnp.int32, (members, members), 1)
    diagonal = row_iota == column_iota
    system = sys_ref[...] + jnp.where(diagonal, 1.0, 0.0)
    squares = jnp.sum(jnp.sum(system * system, axis=0, keepdims=True), axis=1, keepdims=True)
    norm_scale = jnp.sqrt(squares)
    start_y = system / norm_scale

    half_size = members // 2
    half_diagonal = diagonal[:half_size, :half_size]
    y, z, t = (yh, yl), (zh, zl), (th, tl)

    def step_of(blocks):
        first, side, last = blocks
        whole = jnp.where(half_diagonal, 1.5, 0.0)
        return whole - 0.5 * first, -0.5 * side, whole - 0.5 * last

    zh[...], zl[...] = halves(jnp.where(diagonal, 1.5, 0.0) - 0.5 * start_y)
    th[...], tl[...] = halves(start_y)
    keep_product(y, product(z, t))

    def turn(_, carry):
        keep_product(t, step_of(product(z, y)))
        next_y, next_z = product(t, y), product(t, z)
        keep_product(y, next_y)
        keep_product(z, next_z)
        return carry

    lax.fori_loop(0, NS_ITERS - 2, turn, 0)
    keep_product(t, step_of(product(z, y)))
    first, side, last = product(t, z)
    sys_ref[:half_size, :half_size] = first
    sys_ref[:half_size, half_size:] = side
    sys_ref[half_size:, half_size:] = last
    sys_ref[half_size:, :half_size] = jnp.transpose(side)
    iterate_z = sys_ref[...]
    root = jnp.sqrt(norm_scale)
    dims = ((1,), (0,))
    zs = halves(iterate_z)
    three = thirds(projected)
    sent = contract(three, zs[0], dims) + contract(three, zs[1], dims)
    shift = jnp.sum(sent, axis=0, keepdims=True) / (root * norm_factor)
    weights = (iterate_z / root).astype(BF16)
    combined = jnp.sum(contract(thirds(shift), weights, dims), axis=0, keepdims=True)
    combined = thirds(combined)
    groups, fields, rows, width = anomalies_ref.shape
    load.wait()
    for f in range(fields):
        anomalies = rows_of(anomalies_ref, f)
        mean_shift = jnp.sum(contract(combined, anomalies, dims), axis=0, keepdims=True)
        base = mean_ref[f : f + 1, :] + mean_shift
        updated = contract(weights, anomalies, dims)
        o_ref[:, f] = (base + updated).astype(BF16).reshape(groups, rows, width)


def far(a):
    return pltpu.with_memory_space_constraint(a, pltpu.HBM)


def near(a):
    return pltpu.with_memory_space_constraint(a, pltpu.VMEM)


def total_along(part, axis):
    size = lax.axis_size(axis)
    assert size == 8

    def moved(a, shift):
        return lax.ppermute(a, axis, [(i, (i + shift) % size) for i in range(size)])

    before, after = moved(part, 1), moved(part, -1)
    two = before + part
    three = two + after
    return three + (moved(three, 3) + moved(two, -3))


def local(prior_ensemble, measurement_location, measurement_datum, measurement_spread):
    rows, fields, span = prior_ensemble.shape
    peers = lax.axis_size(MEM)
    members = rows * peers
    width = span // peers
    core = lax.axis_index("mem_2").reshape(1).astype(jnp.int32)
    parts = 4
    staging = [pltpu.VMEM((parts, rows, fields, span // parts), BF16), pltpu.SemaphoreType.DMA((parts,))]
    tiled = pltpu.VMEM((peers, fields, rows, width), BF16)
    packed = pl.pallas_call(
        pack_kernel,
        out_shape=pltpu.HBM(tiled.shape, BF16),
        in_specs=[HBM],
        out_specs=HBM,
        scratch_shapes=staging + [tiled, pltpu.SemaphoreType.DMA((parts,))],
        compiler_params=pltpu.CompilerParams(vmem_limit_bytes=8 << 20),
        name="pack",
    )(far(prior_ensemble))
    sites = span * lax.axis_size("cell")
    block_start = (lax.axis_index("cell") * peers + lax.axis_index(MEM)) * width
    block_start = block_start.reshape(1).astype(jnp.int32)
    packed, core, block_start = lax.optimization_barrier((packed, core, block_start))
    state = near(lax.all_to_all(packed, MEM, 0, 0, tiled=True))
    plane = lax.axis_size(PLANE)
    share = -(-len(tiles_of(members)) // (2 * plane))
    half = pltpu.VMEM((share * plane, 8, 128), F32)
    both = pltpu.VMEM((2 * share * plane, 8, 128), F32)
    keep, send = pl.pallas_call(
        functools.partial(gram_kernel, sites=sites),
        out_shape=(half, half),
        in_specs=[SMEM, SMEM, VMEM, VMEM, VMEM, VMEM],
        out_specs=(VMEM, VMEM),
        scratch_shapes=[both],
        compiler_params=pltpu.CompilerParams(vmem_limit_bytes=24 << 20),
        name="gram",
    )(core, block_start, measurement_location, measurement_datum, measurement_spread, state)
    swap = [(0, 1), (1, 0)]
    part = keep + lax.ppermute(send, "mem_2", swap)
    part = lax.all_to_all(part, PLANE, 0, 0, tiled=True)
    part = jnp.sum(part.reshape(plane, share, 8, 128), axis=0)
    anomalies, mean = pl.pallas_call(
        mean_kernel,
        out_shape=(pltpu.HBM(tiled.shape, BF16), pltpu.VMEM((fields, width), F32)),
        in_specs=[VMEM],
        out_specs=(VMEM, VMEM),
        compiler_params=pltpu.CompilerParams(vmem_limit_bytes=24 << 20),
        name="mean",
    )(state)
    part, anomalies, mean = lax.optimization_barrier((part, anomalies, mean))
    part = total_along(part, "cell")
    part = jnp.broadcast_to(part[None], (plane, *part.shape)).reshape(half.shape)
    own = lax.all_to_all(part, PLANE, 0, 0, tiled=True)
    other = lax.ppermute(own, "mem_2", swap)
    square = pltpu.VMEM((members, members), BF16)
    whole = pltpu.VMEM((members, members), F32)
    analysis = pl.pallas_call(
        analysis_kernel,
        out_shape=tiled,
        in_specs=[SMEM, VMEM, VMEM, HBM, VMEM],
        out_specs=VMEM,
        scratch_shapes=[tiled, pltpu.SemaphoreType.DMA, both, whole] + [square] * 6,
        compiler_params=pltpu.CompilerParams(vmem_limit_bytes=32 << 20),
        name="analysis",
    )(core, near(own), near(other), far(anomalies), near(mean))
    returned = lax.all_to_all(analysis, MEM, 0, 0, tiled=True)
    return pl.pallas_call(
        unpack_kernel,
        out_shape=jax.ShapeDtypeStruct(prior_ensemble.shape, BF16),
        in_specs=[VMEM],
        out_specs=HBM,
        scratch_shapes=staging,
        compiler_params=pltpu.CompilerParams(vmem_limit_bytes=8 << 20),
        name="unpack",
    )(near(returned))


def solution(mesh):
    torus = Mesh(
        mesh.devices.reshape(4, 4, 2, mesh.shape["cell"]), ("mem_0", "mem_1", "mem_2", "cell")
    )
    in_specs = (P(MEM, None, "cell"), P("cell", MEM), P("cell", MEM), P("cell", MEM))
    out_specs = P(MEM, None, "cell")
    return jax.shard_map(local, mesh=torus, in_specs=in_specs, out_specs=out_specs, check_vma=False)
```

```python
import functools
import math

import jax
import jax.numpy as jnp
from jax import lax
from jax.experimental import pallas as pl
from jax.experimental.pallas import tpu as pltpu
from jax.sharding import Mesh
from jax.sharding import PartitionSpec as P

NS_ITERS = 8
MEM = ("mem_0", "mem_1", "mem_2")
PLANE = ("mem_0", "mem_1")
F32 = jnp.float32
BF16 = jnp.bfloat16
VMEM = pl.BlockSpec(memory_space=pltpu.VMEM)
HBM = pl.BlockSpec(memory_space=pltpu.HBM)
SMEM = pl.BlockSpec(memory_space=pltpu.SMEM)


def pack_kernel(x_ref, o_ref, buffer, sem, packed, sent):
    parts, width = buffer.shape[0], o_ref.shape[3]
    span = buffer.shape[3]
    each = span // width
    copies = [
        pltpu.make_async_copy(x_ref.at[:, :, pl.ds(i * span, span)], buffer.at[i], sem.at[i])
        for i in range(parts)
    ]
    for c in copies:
        c.start()
    results = [
        pltpu.make_async_copy(
            packed.at[pl.ds(i * each, each)], o_ref.at[pl.ds(i * each, each)], sent.at[i]
        )
        for i in range(parts)
    ]
    for i in range(parts):
        copies[i].wait()
        for k in range(each):
            block = buffer[i, :, :, k * width : (k + 1) * width]
            packed[i * each + k] = jnp.transpose(block, (1, 0, 2))
        results[i].start()
    for c in results:
        c.wait()


def unpack_kernel(y_ref, o_ref, buffer, sem):
    parts, width = buffer.shape[0], y_ref.shape[3]
    span = buffer.shape[3]
    each = span // width
    copies = []
    for i in range(parts):
        for k in range(each):
            block = jnp.transpose(y_ref[i * each + k], (1, 0, 2))
            buffer[i, :, :, k * width : (k + 1) * width] = block
        copy = pltpu.make_async_copy(
            buffer.at[i], o_ref.at[:, :, pl.ds(i * span, span)], sem.at[i]
        )
        copy.start()
        copies.append(copy)
    for c in copies:
        c.wait()


def tiles_of(members):
    blocks = members // 128
    return [
        (row * 128 + i * 8, column * 128)
        for row in range(blocks)
        for column in range(row, blocks)
        for i in range(16)
    ]


def rows_of(x_ref, f):
    groups, _, rows, width = x_ref.shape
    return x_ref[:, f].reshape(groups * rows, width)


def contract(a, b, dims):
    return lax.dot_general(a, b, (dims, ((), ())), preferred_element_type=F32)


def gram_kernel(
    core_ref, start_ref, location_ref, datum_ref, spread_ref, x_ref, keep_ref, send_ref, sum_ref, *, sites
):
    groups, fields, rows, width = x_ref.shape
    members = groups * rows
    norm_factor = math.sqrt(members - 1)
    scaled_parts, innovation_parts = [], []
    iota = lax.broadcasted_iota(jnp.int32, (width, 256), 0)

    def pair(ref, r):
        return jnp.concatenate([ref[r : r + 1, :], ref[r + 1 : r + 2, :]], axis=1)

    start = start_ref[0]
    for r in range(0, location_ref.shape[0], 2):
        location = pair(location_ref, r)
        picked = None
        for f in range(fields):
            chosen = jnp.where(iota == location - (start + f * sites), 1.0, 0.0).astype(BF16)
            term = contract(rows_of(x_ref, f), chosen, ((1,), (0,)))
            picked = term if picked is None else picked + term
        mean = jnp.sum(picked, axis=0, keepdims=True) / members
        anomaly = (picked - mean).astype(BF16).astype(F32)
        error = pair(spread_ref, r)
        scaled_parts.append((anomaly / (error * norm_factor)).astype(BF16))
        innovation_parts.append(((pair(datum_ref, r) - mean) / error).astype(BF16))
    scaled = jnp.concatenate(scaled_parts, axis=1)
    innovation = jnp.concatenate(innovation_parts, axis=1).astype(F32)
    innovation = jnp.broadcast_to(innovation, (16, innovation.shape[1])).astype(BF16)
    gram = contract(scaled, scaled, ((1,), (1,)))
    projected = contract(innovation, scaled, ((1,), (1,)))
    tiles = tiles_of(members)
    for t, (row, column) in enumerate(tiles):
        sum_ref[t] = gram[row : row + 8, column : column + 128]
    rows = jnp.concatenate(
        [projected[0:1, j * 128 : (j + 1) * 128] for j in range(members // 128)], axis=0
    )
    rows = jnp.concatenate([rows, pltpu.roll(rows, 64, 1)], axis=0)
    low_lanes = lax.broadcasted_iota(jnp.int32, rows.shape, 1) < 64
    sum_ref[len(tiles) - 1] = jnp.where(low_lanes, rows, sum_ref[len(tiles) - 1])
    core = core_ref[0]
    half = keep_ref.shape[0]
    keep_ref[...] = sum_ref[pl.ds(core * half, half)]
    send_ref[...] = sum_ref[pl.ds((1 - core) * half, half)]


def mean_kernel(x_ref, anomalies_ref, mean_ref):
    groups, fields, rows, width = x_ref.shape
    members = groups * rows
    for f in range(fields):
        x = x_ref[:, f].astype(F32)
        mean = jnp.sum(jnp.sum(x, axis=0), axis=0, keepdims=True) / members
        mean_ref[f : f + 1, :] = mean
        anomalies_ref[:, f] = (x - mean[None]).astype(BF16)


def halves(a):
    high = a.astype(BF16)
    return high, (a - high.astype(F32)).astype(BF16)


def thirds(row):
    high = row.astype(BF16).astype(F32)
    rest = row - high
    middle = rest.astype(BF16).astype(F32)
    low = rest - middle
    pad = jnp.zeros((13, row.shape[1]), F32)
    return jnp.concatenate([high, middle, low, pad], axis=0).astype(BF16)


def product(a, b):
    size = a[0].shape[0]
    half = size // 2
    dims = ((1,), (0,))

    def block(r, c):
        ah, al = (m[r : r + half, :] for m in a)
        bh, bl = (m[:, c : c + half] for m in b)
        return contract(ah, bh, dims) + (contract(ah, bl, dims) + contract(al, bh, dims))

    return block(0, 0), block(0, half), block(half, half)


def keep_product(pair, blocks):
    high_ref, low_ref = pair
    half = high_ref.shape[0] // 2
    first, side, last = blocks
    places = ((0, 0, first), (0, half, side), (half, half, last), (half, 0, jnp.transpose(side)))
    for r, c, value in places:
        high, low = halves(value)
        high_ref[r : r + half, c : c + half] = high
        low_ref[r : r + half, c : c + half] = low


def analysis_kernel(
    core_ref,
    own_ref,
    other_ref,
    source_ref,
    mean_ref,
    o_ref,
    anomalies_ref,
    sem,
    sum_ref,
    sys_ref,
    yh,
    yl,
    zh,
    zl,
    th,
    tl,
):
    load = pltpu.make_async_copy(source_ref, anomalies_ref, sem)
    load.start()
    members = sys_ref.shape[0]
    norm_factor = math.sqrt(members - 1)
    blocks = members // 128
    core = core_ref[0]
    half = own_ref.shape[0]
    sum_ref[pl.ds(core * half, half)] = own_ref[...]
    sum_ref[pl.ds((1 - core) * half, half)] = other_ref[...]
    tiles = tiles_of(members)
    for t, (row, column) in enumerate(tiles):
        sys_ref[row : row + 8, column : column + 128] = sum_ref[t]
    for i in range(blocks):
        for j in range(i + 1, blocks):
            upper = sys_ref[i * 128 : i * 128 + 128, j * 128 : j * 128 + 128]
            sys_ref[j * 128 : j * 128 + 128, i * 128 : i * 128 + 128] = jnp.transpose(upper)
    tile = sum_ref[len(tiles) - 1]
    low_lanes = lax.broadcasted_iota(jnp.int32, (blocks, 128), 1) < 64
    projected = jnp.where(low_lanes, tile[0:blocks], pltpu.roll(tile[blocks : 2 * blocks], 64, 1))
    projected = jnp.concatenate([projected[j : j + 1, :] for j in range(blocks)], axis=1)
    corner = sys_ref[members - 128 :, members - 128 :]
    low_lanes = lax.broadcasted_iota(jnp.int32, tile.shape, 1) < 64
    sys_ref[members - 8 :, members - 128 :] = jnp.where(low_lanes, jnp.transpose(corner)[120:128], tile)
    row_iota = lax.broadcasted_iota(jnp.int32, (members, members), 0)
    column_iota = lax.broadcasted_iota(jnp.int32, (members, members), 1)
    diagonal = row_iota == column_iota
    system = sys_ref[...] + jnp.where(diagonal, 1.0, 0.0)
    squares = jnp.sum(jnp.sum(system * system, axis=0, keepdims=True), axis=1, keepdims=True)
    norm_scale = jnp.sqrt(squares)
    start_y = system / norm_scale

    half_size = members // 2
    half_diagonal = diagonal[:half_size, :half_size]
    y, z, t = (yh, yl), (zh, zl), (th, tl)

    def step_of(blocks):
        first, side, last = blocks
        whole = jnp.where(half_diagonal, 1.5, 0.0)
        return whole - 0.5 * first, -0.5 * side, whole - 0.5 * last

    zh[...], zl[...] = halves(jnp.where(diagonal, 1.5, 0.0) - 0.5 * start_y)
    th[...], tl[...] = halves(start_y)
    keep_product(y, product(z, t))

    def turn(_, carry):
        keep_product(t, step_of(product(z, y)))
        next_y, next_z = product(t, y), product(t, z)
        keep_product(y, next_y)
        keep_product(z, next_z)
        return carry

    lax.fori_loop(0, NS_ITERS - 2, turn, 0)
    keep_product(t, step_of(product(z, y)))
    first, side, last = product(t, z)
    sys_ref[:half_size, :half_size] = first
    sys_ref[:half_size, half_size:] = side
    sys_ref[half_size:, half_size:] = last
    sys_ref[half_size:, :half_size] = jnp.transpose(side)
    iterate_z = sys_ref[...]
    root = jnp.sqrt(norm_scale)
    dims = ((1,), (0,))
    zs = halves(iterate_z)
    three = thirds(projected)
    sent = contract(three, zs[0], dims) + contract(three, zs[1], dims)
    shift = jnp.sum(sent, axis=0, keepdims=True) / (root * norm_factor)
    weights = (iterate_z / root).astype(BF16)
    combined = jnp.sum(contract(thirds(shift), weights, dims), axis=0, keepdims=True)
    combined = thirds(combined)
    groups, fields, rows, width = anomalies_ref.shape
    load.wait()
    for f in range(fields):
        anomalies = rows_of(anomalies_ref, f)
        mean_shift = jnp.sum(contract(combined, anomalies, dims), axis=0, keepdims=True)
        base = mean_ref[f : f + 1, :] + mean_shift
        updated = contract(weights, anomalies, dims)
        o_ref[:, f] = (base + updated).astype(BF16).reshape(groups, rows, width)


def far(a):
    return pltpu.with_memory_space_constraint(a, pltpu.HBM)


def near(a):
    return pltpu.with_memory_space_constraint(a, pltpu.VMEM)


def spread(part, peers):
    return jnp.broadcast_to(part[None], (peers, *part.shape)).reshape(-1, *part.shape[1:])


def summed(part, peers):
    return jnp.sum(part.reshape(peers, -1, *part.shape[1:]), axis=0)


def local(prior_ensemble, measurement_location, measurement_datum, measurement_spread):
    rows, fields, span = prior_ensemble.shape
    peers = lax.axis_size(MEM)
    members = rows * peers
    width = span // peers
    core = lax.axis_index("mem_2").reshape(1).astype(jnp.int32)
    parts = 4
    staging = [pltpu.VMEM((parts, rows, fields, span // parts), BF16), pltpu.SemaphoreType.DMA((parts,))]
    tiled = pltpu.VMEM((peers, fields, rows, width), BF16)
    packed = pl.pallas_call(
        pack_kernel,
        out_shape=pltpu.HBM(tiled.shape, BF16),
        in_specs=[HBM],
        out_specs=HBM,
        scratch_shapes=staging + [tiled, pltpu.SemaphoreType.DMA((parts,))],
        compiler_params=pltpu.CompilerParams(vmem_limit_bytes=8 << 20),
        name="pack",
    )(far(prior_ensemble))
    sites = span * lax.axis_size("cell")
    block_start = (lax.axis_index("cell") * peers + lax.axis_index(MEM)) * width
    block_start = block_start.reshape(1).astype(jnp.int32)
    packed, core, block_start = lax.optimization_barrier((packed, core, block_start))
    state = near(lax.all_to_all(packed, MEM, 0, 0, tiled=True))
    plane = lax.axis_size(PLANE)
    share = -(-len(tiles_of(members)) // (2 * plane))
    half = pltpu.VMEM((share * plane, 8, 128), F32)
    both = pltpu.VMEM((2 * share * plane, 8, 128), F32)
    keep, send = pl.pallas_call(
        functools.partial(gram_kernel, sites=sites),
        out_shape=(half, half),
        in_specs=[SMEM, SMEM, VMEM, VMEM, VMEM, VMEM],
        out_specs=(VMEM, VMEM),
        scratch_shapes=[both],
        compiler_params=pltpu.CompilerParams(vmem_limit_bytes=24 << 20),
        name="gram",
    )(core, block_start, measurement_location, measurement_datum, measurement_spread, state)
    swap = [(0, 1), (1, 0)]
    part = keep + lax.ppermute(send, "mem_2", swap)
    part = lax.all_to_all(part, PLANE, 0, 0, tiled=True)
    part = summed(part, plane)
    planes = lax.axis_size("cell")
    part = summed(lax.all_to_all(spread(part, planes), "cell", 0, 0, tiled=True), planes)
    anomalies, mean = pl.pallas_call(
        mean_kernel,
        out_shape=(pltpu.HBM(tiled.shape, BF16), pltpu.VMEM((fields, width), F32)),
        in_specs=[VMEM],
        out_specs=(VMEM, VMEM),
        compiler_params=pltpu.CompilerParams(vmem_limit_bytes=24 << 20),
        name="mean",
    )(state)
    part, anomalies, mean = lax.optimization_barrier((part, anomalies, mean))
    own = lax.all_to_all(spread(part, plane), PLANE, 0, 0, tiled=True)
    other = lax.ppermute(own, "mem_2", swap)
    square = pltpu.VMEM((members, members), BF16)
    whole = pltpu.VMEM((members, members), F32)
    analysis = pl.pallas_call(
        analysis_kernel,
        out_shape=tiled,
        in_specs=[SMEM, VMEM, VMEM, HBM, VMEM],
        out_specs=VMEM,
        scratch_shapes=[tiled, pltpu.SemaphoreType.DMA, both, whole] + [square] * 6,
        compiler_params=pltpu.CompilerParams(vmem_limit_bytes=32 << 20),
        name="analysis",
    )(core, near(own), near(other), far(anomalies), near(mean))
    returned = lax.all_to_all(analysis, MEM, 0, 0, tiled=True)
    return pl.pallas_call(
        unpack_kernel,
        out_shape=jax.ShapeDtypeStruct(prior_ensemble.shape, BF16),
        in_specs=[VMEM],
        out_specs=HBM,
        scratch_shapes=staging,
        compiler_params=pltpu.CompilerParams(vmem_limit_bytes=8 << 20),
        name="unpack",
    )(near(returned))


def solution(mesh):
    torus = Mesh(
        mesh.devices.reshape(4, 4, 2, mesh.shape["cell"]), ("mem_0", "mem_1", "mem_2", "cell")
    )
    in_specs = (P(MEM, None, "cell"), P("cell", MEM), P("cell", MEM), P("cell", MEM))
    out_specs = P(MEM, None, "cell")
    return jax.shard_map(local, mesh=torus, in_specs=in_specs, out_specs=out_specs, check_vma=False)
```

```python
import functools
import math

import jax
import jax.numpy as jnp
from jax import lax
from jax.experimental import pallas as pl
from jax.experimental.pallas import tpu as pltpu
from jax.sharding import Mesh
from jax.sharding import PartitionSpec as P

NS_ITERS = 8
MEM = ("mem_0", "mem_1", "mem_2")
PLANE = ("mem_0", "mem_1")
F32 = jnp.float32
BF16 = jnp.bfloat16
VMEM = pl.BlockSpec(memory_space=pltpu.VMEM)
HBM = pl.BlockSpec(memory_space=pltpu.HBM)
SMEM = pl.BlockSpec(memory_space=pltpu.SMEM)


def pack_kernel(x_ref, o_ref, buffer, sem, packed, sent):
    parts, width = buffer.shape[0], o_ref.shape[3]
    span = buffer.shape[3]
    each = span // width
    copies = [
        pltpu.make_async_copy(x_ref.at[:, :, pl.ds(i * span, span)], buffer.at[i], sem.at[i])
        for i in range(parts)
    ]
    for c in copies:
        c.start()
    results = [
        pltpu.make_async_copy(
            packed.at[pl.ds(i * each, each)], o_ref.at[pl.ds(i * each, each)], sent.at[i]
        )
        for i in range(parts)
    ]
    for i in range(parts):
        copies[i].wait()
        for k in range(each):
            block = buffer[i, :, :, k * width : (k + 1) * width]
            packed[i * each + k] = jnp.transpose(block, (1, 0, 2))
        results[i].start()
    for c in results:
        c.wait()


def unpack_kernel(y_ref, o_ref, buffer, sem):
    parts, width = buffer.shape[0], y_ref.shape[3]
    span = buffer.shape[3]
    each = span // width
    copies = []
    for i in range(parts):
        for k in range(each):
            block = jnp.transpose(y_ref[i * each + k], (1, 0, 2))
            buffer[i, :, :, k * width : (k + 1) * width] = block
        copy = pltpu.make_async_copy(
            buffer.at[i], o_ref.at[:, :, pl.ds(i * span, span)], sem.at[i]
        )
        copy.start()
        copies.append(copy)
    for c in copies:
        c.wait()


def tiles_of(members):
    blocks = members // 128
    return [
        (row * 128 + i * 8, column * 128)
        for row in range(blocks)
        for column in range(row, blocks)
        for i in range(16)
    ]


def rows_of(x_ref, f):
    groups, _, rows, width = x_ref.shape
    return x_ref[:, f].reshape(groups * rows, width)


def contract(a, b, dims):
    return lax.dot_general(a, b, (dims, ((), ())), preferred_element_type=F32)


def gram_kernel(
    core_ref, start_ref, location_ref, datum_ref, spread_ref, x_ref, keep_ref, send_ref, sum_ref, *, sites
):
    groups, fields, rows, width = x_ref.shape
    members = groups * rows
    norm_factor = math.sqrt(members - 1)
    scaled_parts, innovation_parts = [], []
    iota = lax.broadcasted_iota(jnp.int32, (width, 256), 0)

    def pair(ref, r):
        return jnp.concatenate([ref[r : r + 1, :], ref[r + 1 : r + 2, :]], axis=1)

    start = start_ref[0]
    for r in range(0, location_ref.shape[0], 2):
        location = pair(location_ref, r)
        picked = None
        for f in range(fields):
            chosen = jnp.where(iota == location - (start + f * sites), 1.0, 0.0).astype(BF16)
            term = contract(rows_of(x_ref, f), chosen, ((1,), (0,)))
            picked = term if picked is None else picked + term
        mean = jnp.sum(picked, axis=0, keepdims=True) / members
        anomaly = (picked - mean).astype(BF16).astype(F32)
        error = pair(spread_ref, r)
        scaled_parts.append((anomaly / (error * norm_factor)).astype(BF16))
        innovation_parts.append(((pair(datum_ref, r) - mean) / error).astype(BF16))
    scaled = jnp.concatenate(scaled_parts, axis=1)
    innovation = jnp.concatenate(innovation_parts, axis=1).astype(F32)
    innovation = jnp.broadcast_to(innovation, (16, innovation.shape[1])).astype(BF16)
    gram = contract(scaled, scaled, ((1,), (1,)))
    projected = contract(innovation, scaled, ((1,), (1,)))
    tiles = tiles_of(members)
    for t, (row, column) in enumerate(tiles):
        sum_ref[t] = gram[row : row + 8, column : column + 128]
    rows = jnp.concatenate(
        [projected[0:1, j * 128 : (j + 1) * 128] for j in range(members // 128)], axis=0
    )
    rows = jnp.concatenate([rows, pltpu.roll(rows, 64, 1)], axis=0)
    low_lanes = lax.broadcasted_iota(jnp.int32, rows.shape, 1) < 64
    sum_ref[len(tiles) - 1] = jnp.where(low_lanes, rows, sum_ref[len(tiles) - 1])
    core = core_ref[0]
    half = keep_ref.shape[0]
    keep_ref[...] = sum_ref[pl.ds(core * half, half)]
    send_ref[...] = sum_ref[pl.ds((1 - core) * half, half)]


def mean_kernel(x_ref, anomalies_ref, mean_ref):
    groups, fields, rows, width = x_ref.shape
    members = groups * rows
    for f in range(fields):
        x = x_ref[:, f].astype(F32)
        mean = jnp.sum(jnp.sum(x, axis=0), axis=0, keepdims=True) / members
        mean_ref[f : f + 1, :] = mean
        anomalies_ref[:, f] = (x - mean[None]).astype(BF16)


def halves(a):
    high = a.astype(BF16)
    return high, (a - high.astype(F32)).astype(BF16)


def thirds(row):
    high = row.astype(BF16).astype(F32)
    rest = row - high
    middle = rest.astype(BF16).astype(F32)
    low = rest - middle
    pad = jnp.zeros((13, row.shape[1]), F32)
    return jnp.concatenate([high, middle, low, pad], axis=0).astype(BF16)


def product(a, b):
    size = a[0].shape[0]
    half = size // 2
    dims = ((1,), (0,))

    def block(r, c):
        ah, al = (m[r : r + half, :] for m in a)
        bh, bl = (m[:, c : c + half] for m in b)
        return contract(ah, bh, dims) + (contract(ah, bl, dims) + contract(al, bh, dims))

    return block(0, 0), block(0, half), block(half, half)


def keep_product(pair, blocks):
    high_ref, low_ref = pair
    half = high_ref.shape[0] // 2
    first, side, last = blocks
    places = ((0, 0, first), (0, half, side), (half, half, last), (half, 0, jnp.transpose(side)))
    for r, c, value in places:
        high, low = halves(value)
        high_ref[r : r + half, c : c + half] = high
        low_ref[r : r + half, c : c + half] = low


def analysis_kernel(
    core_ref,
    own_ref,
    other_ref,
    anomalies_ref,
    mean_ref,
    o_ref,
    sum_ref,
    sys_ref,
    yh,
    yl,
    zh,
    zl,
    th,
    tl,
):
    members = sys_ref.shape[0]
    norm_factor = math.sqrt(members - 1)
    blocks = members // 128
    core = core_ref[0]
    half = own_ref.shape[0]
    sum_ref[pl.ds(core * half, half)] = own_ref[...]
    sum_ref[pl.ds((1 - core) * half, half)] = other_ref[...]
    tiles = tiles_of(members)
    for t, (row, column) in enumerate(tiles):
        sys_ref[row : row + 8, column : column + 128] = sum_ref[t]
    for i in range(blocks):
        for j in range(i + 1, blocks):
            upper = sys_ref[i * 128 : i * 128 + 128, j * 128 : j * 128 + 128]
            sys_ref[j * 128 : j * 128 + 128, i * 128 : i * 128 + 128] = jnp.transpose(upper)
    tile = sum_ref[len(tiles) - 1]
    low_lanes = lax.broadcasted_iota(jnp.int32, (blocks, 128), 1) < 64
    projected = jnp.where(low_lanes, tile[0:blocks], pltpu.roll(tile[blocks : 2 * blocks], 64, 1))
    projected = jnp.concatenate([projected[j : j + 1, :] for j in range(blocks)], axis=1)
    corner = sys_ref[members - 128 :, members - 128 :]
    low_lanes = lax.broadcasted_iota(jnp.int32, tile.shape, 1) < 64
    sys_ref[members - 8 :, members - 128 :] = jnp.where(low_lanes, jnp.transpose(corner)[120:128], tile)
    row_iota = lax.broadcasted_iota(jnp.int32, (members, members), 0)
    column_iota = lax.broadcasted_iota(jnp.int32, (members, members), 1)
    diagonal = row_iota == column_iota
    system = sys_ref[...] + jnp.where(diagonal, 1.0, 0.0)
    squares = jnp.sum(jnp.sum(system * system, axis=0, keepdims=True), axis=1, keepdims=True)
    norm_scale = jnp.sqrt(squares)
    start_y = system / norm_scale

    half_size = members // 2
    half_diagonal = diagonal[:half_size, :half_size]
    y, z, t = (yh, yl), (zh, zl), (th, tl)

    def step_of(blocks):
        first, side, last = blocks
        whole = jnp.where(half_diagonal, 1.5, 0.0)
        return whole - 0.5 * first, -0.5 * side, whole - 0.5 * last

    zh[...], zl[...] = halves(jnp.where(diagonal, 1.5, 0.0) - 0.5 * start_y)
    th[...], tl[...] = halves(start_y)
    keep_product(y, product(z, t))

    def turn(_, carry):
        keep_product(t, step_of(product(z, y)))
        next_y, next_z = product(t, y), product(t, z)
        keep_product(y, next_y)
        keep_product(z, next_z)
        return carry

    lax.fori_loop(0, NS_ITERS - 2, turn, 0, unroll=NS_ITERS - 2)
    keep_product(t, step_of(product(z, y)))
    first, side, last = product(t, z)
    sys_ref[:half_size, :half_size] = first
    sys_ref[:half_size, half_size:] = side
    sys_ref[half_size:, half_size:] = last
    sys_ref[half_size:, :half_size] = jnp.transpose(side)
    iterate_z = sys_ref[...]
    root = jnp.sqrt(norm_scale)
    dims = ((1,), (0,))
    zs = halves(iterate_z)
    three = thirds(projected)
    sent = contract(three, zs[0], dims) + contract(three, zs[1], dims)
    shift = jnp.sum(sent, axis=0, keepdims=True) / (root * norm_factor)
    weights = (iterate_z / root).astype(BF16)
    combined = jnp.sum(contract(thirds(shift), weights, dims), axis=0, keepdims=True)
    combined = thirds(combined)
    groups, fields, rows, width = anomalies_ref.shape
    for f in range(fields):
        anomalies = rows_of(anomalies_ref, f)
        mean_shift = jnp.sum(contract(combined, anomalies, dims), axis=0, keepdims=True)
        base = mean_ref[f : f + 1, :] + mean_shift
        updated = contract(weights, anomalies, dims)
        o_ref[:, f] = (base + updated).astype(BF16).reshape(groups, rows, width)


def far(a):
    return pltpu.with_memory_space_constraint(a, pltpu.HBM)


def near(a):
    return pltpu.with_memory_space_constraint(a, pltpu.VMEM)


def spread(part, peers):
    return jnp.broadcast_to(part[None], (peers, *part.shape)).reshape(-1, *part.shape[1:])


def summed(part, peers):
    return jnp.sum(part.reshape(peers, -1, *part.shape[1:]), axis=0)


def local(prior_ensemble, measurement_location, measurement_datum, measurement_spread):
    rows, fields, span = prior_ensemble.shape
    peers = lax.axis_size(MEM)
    members = rows * peers
    width = span // peers
    core = lax.axis_index("mem_2").reshape(1).astype(jnp.int32)
    parts = 4
    staging = [pltpu.VMEM((parts, rows, fields, span // parts), BF16), pltpu.SemaphoreType.DMA((parts,))]
    tiled = pltpu.VMEM((peers, fields, rows, width), BF16)
    packed = pl.pallas_call(
        pack_kernel,
        out_shape=pltpu.HBM(tiled.shape, BF16),
        in_specs=[HBM],
        out_specs=HBM,
        scratch_shapes=staging + [tiled, pltpu.SemaphoreType.DMA((parts,))],
        compiler_params=pltpu.CompilerParams(vmem_limit_bytes=8 << 20),
        name="pack",
    )(far(prior_ensemble))
    sites = span * lax.axis_size("cell")
    block_start = (lax.axis_index("cell") * peers + lax.axis_index(MEM)) * width
    block_start = block_start.reshape(1).astype(jnp.int32)
    packed, core, block_start = lax.optimization_barrier((packed, core, block_start))
    state = near(lax.all_to_all(packed, MEM, 0, 0, tiled=True))
    plane = lax.axis_size(PLANE)
    share = -(-len(tiles_of(members)) // (2 * plane))
    half = pltpu.VMEM((share * plane, 8, 128), F32)
    both = pltpu.VMEM((2 * share * plane, 8, 128), F32)
    keep, send = pl.pallas_call(
        functools.partial(gram_kernel, sites=sites),
        out_shape=(half, half),
        in_specs=[SMEM, SMEM, VMEM, VMEM, VMEM, VMEM],
        out_specs=(VMEM, VMEM),
        scratch_shapes=[both],
        compiler_params=pltpu.CompilerParams(vmem_limit_bytes=24 << 20),
        name="gram",
    )(core, block_start, measurement_location, measurement_datum, measurement_spread, state)
    swap = [(0, 1), (1, 0)]
    part = keep + lax.ppermute(send, "mem_2", swap)
    part = lax.all_to_all(part, PLANE, 0, 0, tiled=True)
    part = summed(part, plane)
    planes = lax.axis_size("cell")
    part = summed(lax.all_to_all(spread(part, planes), "cell", 0, 0, tiled=True), planes)
    anomalies, mean = pl.pallas_call(
        mean_kernel,
        out_shape=(tiled, pltpu.VMEM((fields, width), F32)),
        input_output_aliases={0: 0},
        in_specs=[VMEM],
        out_specs=(VMEM, VMEM),
        compiler_params=pltpu.CompilerParams(vmem_limit_bytes=24 << 20),
        name="mean",
    )(state)
    own = lax.all_to_all(spread(part, plane), PLANE, 0, 0, tiled=True)
    other = lax.ppermute(own, "mem_2", swap)
    square = pltpu.VMEM((members, members), BF16)
    whole = pltpu.VMEM((members, members), F32)
    analysis = pl.pallas_call(
        analysis_kernel,
        out_shape=tiled,
        in_specs=[SMEM, VMEM, VMEM, VMEM, VMEM],
        out_specs=VMEM,
        scratch_shapes=[both, whole] + [square] * 6,
        compiler_params=pltpu.CompilerParams(vmem_limit_bytes=32 << 20),
        name="analysis",
    )(core, near(own), near(other), near(anomalies), near(mean))
    returned = lax.all_to_all(analysis, MEM, 0, 0, tiled=True)
    return pl.pallas_call(
        unpack_kernel,
        out_shape=jax.ShapeDtypeStruct(prior_ensemble.shape, BF16),
        in_specs=[VMEM],
        out_specs=HBM,
        scratch_shapes=staging,
        compiler_params=pltpu.CompilerParams(vmem_limit_bytes=8 << 20),
        name="unpack",
    )(near(returned))


def solution(mesh):
    torus = Mesh(
        mesh.devices.reshape(4, 4, 2, mesh.shape["cell"]), ("mem_0", "mem_1", "mem_2", "cell")
    )
    in_specs = (P(MEM, None, "cell"), P("cell", MEM), P("cell", MEM), P("cell", MEM))
    out_specs = P(MEM, None, "cell")
    return jax.shard_map(local, mesh=torus, in_specs=in_specs, out_specs=out_specs, check_vma=False)
```

```python
import functools
import math

import jax
import jax.numpy as jnp
from jax import lax
from jax.experimental import pallas as pl
from jax.experimental.pallas import tpu as pltpu
from jax.sharding import Mesh
from jax.sharding import PartitionSpec as P

NS_ITERS = 8
MEM = ("mem_0", "mem_1", "mem_2")
PLANE = ("mem_0", "mem_1")
F32 = jnp.float32
BF16 = jnp.bfloat16
VMEM = pl.BlockSpec(memory_space=pltpu.VMEM)
HBM = pl.BlockSpec(memory_space=pltpu.HBM)
SMEM = pl.BlockSpec(memory_space=pltpu.SMEM)


def pack_kernel(x_ref, o_ref, buffer, sem, packed, sent):
    parts, width = buffer.shape[0], o_ref.shape[3]
    span = buffer.shape[3]
    each = span // width
    copies = [
        pltpu.make_async_copy(x_ref.at[:, :, pl.ds(i * span, span)], buffer.at[i], sem.at[i])
        for i in range(parts)
    ]
    for c in copies:
        c.start()
    results = [
        pltpu.make_async_copy(
            packed.at[pl.ds(i * each, each)], o_ref.at[pl.ds(i * each, each)], sent.at[i]
        )
        for i in range(parts)
    ]
    for i in range(parts):
        copies[i].wait()
        for k in range(each):
            block = buffer[i, :, :, k * width : (k + 1) * width]
            packed[i * each + k] = jnp.transpose(block, (1, 0, 2))
        results[i].start()
    for c in results:
        c.wait()


def unpack_kernel(y_ref, o_ref, buffer, sem):
    parts, width = buffer.shape[0], y_ref.shape[3]
    span = buffer.shape[3]
    each = span // width
    copies = []
    for i in range(parts):
        for k in range(each):
            block = jnp.transpose(y_ref[i * each + k], (1, 0, 2))
            buffer[i, :, :, k * width : (k + 1) * width] = block
        copy = pltpu.make_async_copy(
            buffer.at[i], o_ref.at[:, :, pl.ds(i * span, span)], sem.at[i]
        )
        copy.start()
        copies.append(copy)
    for c in copies:
        c.wait()


def tiles_of(members):
    blocks = members // 128
    return [
        (row * 128 + i * 8, column * 128)
        for row in range(blocks)
        for column in range(row, blocks)
        for i in range(16)
    ]


def rows_of(x_ref, f):
    groups, _, rows, width = x_ref.shape
    return x_ref[:, f].reshape(groups * rows, width)


def contract(a, b, dims):
    return lax.dot_general(a, b, (dims, ((), ())), preferred_element_type=F32)


def gram_kernel(
    core_ref, start_ref, location_ref, datum_ref, spread_ref, x_ref, keep_ref, send_ref, sum_ref, *, sites
):
    groups, fields, rows, width = x_ref.shape
    members = groups * rows
    norm_factor = math.sqrt(members - 1)
    scaled_parts, innovation_parts = [], []
    iota = lax.broadcasted_iota(jnp.int32, (width, 256), 0)

    def pair(ref, r):
        return jnp.concatenate([ref[r : r + 1, :], ref[r + 1 : r + 2, :]], axis=1)

    start = start_ref[0]
    for r in range(0, location_ref.shape[0], 2):
        location = pair(location_ref, r)
        picked = None
        for f in range(fields):
            chosen = jnp.where(iota == location - (start + f * sites), 1.0, 0.0).astype(BF16)
            term = contract(rows_of(x_ref, f), chosen, ((1,), (0,)))
            picked = term if picked is None else picked + term
        mean = jnp.sum(picked, axis=0, keepdims=True) / members
        anomaly = (picked - mean).astype(BF16).astype(F32)
        error = pair(spread_ref, r)
        scaled_parts.append((anomaly * (1.0 / (error * norm_factor))).astype(BF16))
        innovation_parts.append(((pair(datum_ref, r) - mean) / error).astype(BF16))
    scaled = jnp.concatenate(scaled_parts, axis=1)
    innovation = jnp.concatenate(innovation_parts, axis=1).astype(F32)
    innovation = jnp.broadcast_to(innovation, (16, innovation.shape[1])).astype(BF16)
    gram = contract(scaled, scaled, ((1,), (1,)))
    projected = contract(innovation, scaled, ((1,), (1,)))
    tiles = tiles_of(members)
    for t, (row, column) in enumerate(tiles):
        sum_ref[t] = gram[row : row + 8, column : column + 128]
    rows = jnp.concatenate(
        [projected[0:1, j * 128 : (j + 1) * 128] for j in range(members // 128)], axis=0
    )
    rows = jnp.concatenate([rows, pltpu.roll(rows, 64, 1)], axis=0)
    low_lanes = lax.broadcasted_iota(jnp.int32, rows.shape, 1) < 64
    sum_ref[len(tiles) - 1] = jnp.where(low_lanes, rows, sum_ref[len(tiles) - 1])
    core = core_ref[0]
    half = keep_ref.shape[0]
    keep_ref[...] = sum_ref[pl.ds(core * half, half)]
    send_ref[...] = sum_ref[pl.ds((1 - core) * half, half)]


def mean_kernel(x_ref, anomalies_ref, mean_ref):
    groups, fields, rows, width = x_ref.shape
    members = groups * rows
    for f in range(fields):
        x = x_ref[:, f].astype(F32)
        mean = jnp.sum(jnp.sum(x, axis=0), axis=0, keepdims=True) / members
        mean_ref[f : f + 1, :] = mean
        anomalies_ref[:, f] = (x - mean[None]).astype(BF16)


def halves(a):
    high = a.astype(BF16)
    return high, (a - high.astype(F32)).astype(BF16)


def thirds(row):
    high = row.astype(BF16).astype(F32)
    rest = row - high
    middle = rest.astype(BF16).astype(F32)
    low = rest - middle
    pad = jnp.zeros((13, row.shape[1]), F32)
    return jnp.concatenate([high, middle, low, pad], axis=0).astype(BF16)


def product(a, b):
    size = a[0].shape[0]
    half = size // 2
    dims = ((1,), (0,))

    def block(r, c):
        ah, al = (m[r : r + half, :] for m in a)
        bh, bl = (m[:, c : c + half] for m in b)
        return contract(ah, bh, dims) + (contract(ah, bl, dims) + contract(al, bh, dims))

    return block(0, 0), block(0, half), block(half, half)


def keep_product(pair, blocks):
    high_ref, low_ref = pair
    half = high_ref.shape[0] // 2
    first, side, last = blocks
    places = ((0, 0, first), (0, half, side), (half, half, last), (half, 0, jnp.transpose(side)))
    for r, c, value in places:
        high, low = halves(value)
        high_ref[r : r + half, c : c + half] = high
        low_ref[r : r + half, c : c + half] = low


def diagonal_of(size):
    rows = lax.broadcasted_iota(jnp.int32, (size, size), 0)
    return rows == lax.broadcasted_iota(jnp.int32, (size, size), 1)


def through(row, pair):
    parts = thirds(row)
    dims = ((1,), (0,))
    sent = contract(parts, pair[0][...], dims) + contract(parts, pair[1][...], dims)
    return jnp.sum(sent, axis=0, keepdims=True)


def analysis_kernel(
    core_ref,
    own_ref,
    other_ref,
    anomalies_ref,
    mean_ref,
    o_ref,
    sum_ref,
    sys_ref,
    yh,
    yl,
    zh,
    zl,
    th,
    tl,
):
    members = sys_ref.shape[0]
    norm_factor = math.sqrt(members - 1)
    blocks = members // 128
    core = core_ref[0]
    half = own_ref.shape[0]
    sum_ref[pl.ds(core * half, half)] = own_ref[...]
    sum_ref[pl.ds((1 - core) * half, half)] = other_ref[...]
    tiles = tiles_of(members)
    for t, (row, column) in enumerate(tiles):
        sys_ref[row : row + 8, column : column + 128] = sum_ref[t]
    tile = sum_ref[len(tiles) - 1]
    low_lanes = lax.broadcasted_iota(jnp.int32, (blocks, 128), 1) < 64
    projected = jnp.where(low_lanes, tile[0:blocks], pltpu.roll(tile[blocks : 2 * blocks], 64, 1))
    projected = jnp.concatenate([projected[j : j + 1, :] for j in range(blocks)], axis=1)
    corner = sys_ref[members - 128 :, members - 128 :]
    low_lanes = lax.broadcasted_iota(jnp.int32, tile.shape, 1) < 64
    sys_ref[members - 8 :, members - 128 :] = jnp.where(low_lanes, jnp.transpose(corner)[120:128], tile)
    squares = jnp.zeros((128, 128), F32)
    unit = jnp.where(diagonal_of(128), 1.0, 0.0)
    for i in range(blocks):
        here = slice(i * 128, i * 128 + 128)
        value = sys_ref[here, here] + unit
        sys_ref[here, here] = value
        squares = squares + value * value
        for j in range(i + 1, blocks):
            there = slice(j * 128, j * 128 + 128)
            value = sys_ref[here, there]
            sys_ref[there, here] = jnp.transpose(value)
            squares = squares + 2.0 * (value * value)
    squares = jnp.sum(jnp.sum(squares, axis=0, keepdims=True), axis=1, keepdims=True)
    norm_scale = jnp.sqrt(squares)
    one_over = 1.0 / norm_scale
    half_size = members // 2
    half_diagonal = diagonal_of(half_size)
    y, z, t = (yh, yl), (zh, zl), (th, tl)

    def step_of(blocks):
        first, side, last = blocks
        whole = jnp.where(half_diagonal, 1.5, 0.0)
        return whole - 0.5 * first, -0.5 * side, whole - 0.5 * last

    for r in (0, half_size):
        for c in (0, half_size):
            here = (slice(r, r + half_size), slice(c, c + half_size))
            value = sys_ref[here] * one_over
            th[here], tl[here] = halves(value)
            base = jnp.where(half_diagonal, 1.5, 0.0) if r == c else 0.0
            zh[here], zl[here] = halves(base - 0.5 * value)
    keep_product(y, product(z, t))

    def turn(_, carry):
        keep_product(t, step_of(product(z, y)))
        next_y, next_z = product(t, y), product(t, z)
        keep_product(y, next_y)
        keep_product(z, next_z)
        return carry

    lax.fori_loop(0, NS_ITERS - 2, turn, 0, unroll=NS_ITERS - 2)
    keep_product(t, step_of(product(z, y)))
    root = jnp.sqrt(norm_scale)
    shift = through(through(projected, t), z) / (root * norm_factor)
    first, side, last = (b * (1.0 / root) for b in product(t, z))
    weights = jnp.concatenate(
        [
            jnp.concatenate([first, side], axis=1),
            jnp.concatenate([jnp.transpose(side), last], axis=1),
        ],
        axis=0,
    ).astype(BF16)
    dims = ((1,), (0,))
    combined = jnp.sum(contract(thirds(shift), weights, dims), axis=0, keepdims=True)
    combined = thirds(combined)
    groups, fields, rows, width = anomalies_ref.shape
    for f in range(fields):
        anomalies = rows_of(anomalies_ref, f)
        mean_shift = jnp.sum(contract(combined, anomalies, dims), axis=0, keepdims=True)
        base = mean_ref[f : f + 1, :] + mean_shift
        updated = contract(weights, anomalies, dims)
        o_ref[:, f] = (base + updated).astype(BF16).reshape(groups, rows, width)


def far(a):
    return pltpu.with_memory_space_constraint(a, pltpu.HBM)


def near(a):
    return pltpu.with_memory_space_constraint(a, pltpu.VMEM)


def spread(part, peers):
    return jnp.broadcast_to(part[None], (peers, *part.shape)).reshape(-1, *part.shape[1:])


def summed(part, peers):
    return jnp.sum(part.reshape(peers, -1, *part.shape[1:]), axis=0)


def local(prior_ensemble, measurement_location, measurement_datum, measurement_spread):
    rows, fields, span = prior_ensemble.shape
    peers = lax.axis_size(MEM)
    members = rows * peers
    width = span // peers
    core = lax.axis_index("mem_2").reshape(1).astype(jnp.int32)
    parts = 4
    staging = [pltpu.VMEM((parts, rows, fields, span // parts), BF16), pltpu.SemaphoreType.DMA((parts,))]
    tiled = pltpu.VMEM((peers, fields, rows, width), BF16)
    packed = pl.pallas_call(
        pack_kernel,
        out_shape=pltpu.HBM(tiled.shape, BF16),
        in_specs=[HBM],
        out_specs=HBM,
        scratch_shapes=staging + [tiled, pltpu.SemaphoreType.DMA((parts,))],
        compiler_params=pltpu.CompilerParams(vmem_limit_bytes=8 << 20),
        name="pack",
    )(far(prior_ensemble))
    sites = span * lax.axis_size("cell")
    block_start = (lax.axis_index("cell") * peers + lax.axis_index(MEM)) * width
    block_start = block_start.reshape(1).astype(jnp.int32)
    packed, core, block_start = lax.optimization_barrier((packed, core, block_start))
    state = near(lax.all_to_all(packed, MEM, 0, 0, tiled=True))
    plane = lax.axis_size(PLANE)
    share = -(-len(tiles_of(members)) // (2 * plane))
    half = pltpu.VMEM((share * plane, 8, 128), F32)
    both = pltpu.VMEM((2 * share * plane, 8, 128), F32)
    keep, send = pl.pallas_call(
        functools.partial(gram_kernel, sites=sites),
        out_shape=(half, half),
        in_specs=[SMEM, SMEM, VMEM, VMEM, VMEM, VMEM],
        out_specs=(VMEM, VMEM),
        scratch_shapes=[both],
        compiler_params=pltpu.CompilerParams(vmem_limit_bytes=24 << 20),
        name="gram",
    )(core, block_start, measurement_location, measurement_datum, measurement_spread, state)
    swap = [(0, 1), (1, 0)]
    part = keep + lax.ppermute(send, "mem_2", swap)
    part = lax.all_to_all(part, PLANE, 0, 0, tiled=True)
    part = summed(part, plane)
    planes = lax.axis_size("cell")
    part = summed(lax.all_to_all(spread(part, planes), "cell", 0, 0, tiled=True), planes)
    anomalies, mean = pl.pallas_call(
        mean_kernel,
        out_shape=(tiled, pltpu.VMEM((fields, width), F32)),
        input_output_aliases={0: 0},
        in_specs=[VMEM],
        out_specs=(VMEM, VMEM),
        compiler_params=pltpu.CompilerParams(vmem_limit_bytes=24 << 20),
        name="mean",
    )(state)
    own = lax.all_to_all(spread(part, plane), PLANE, 0, 0, tiled=True)
    other = lax.ppermute(own, "mem_2", swap)
    square = pltpu.VMEM((members, members), BF16)
    whole = pltpu.VMEM((members, members), F32)
    analysis = pl.pallas_call(
        analysis_kernel,
        out_shape=tiled,
        in_specs=[SMEM, VMEM, VMEM, VMEM, VMEM],
        out_specs=VMEM,
        scratch_shapes=[both, whole] + [square] * 6,
        compiler_params=pltpu.CompilerParams(vmem_limit_bytes=32 << 20),
        name="analysis",
    )(core, near(own), near(other), near(anomalies), near(mean))
    returned = lax.all_to_all(analysis, MEM, 0, 0, tiled=True)
    return pl.pallas_call(
        unpack_kernel,
        out_shape=jax.ShapeDtypeStruct(prior_ensemble.shape, BF16),
        in_specs=[VMEM],
        out_specs=HBM,
        scratch_shapes=staging,
        compiler_params=pltpu.CompilerParams(vmem_limit_bytes=8 << 20),
        name="unpack",
    )(near(returned))


def solution(mesh):
    torus = Mesh(
        mesh.devices.reshape(4, 4, 2, mesh.shape["cell"]), ("mem_0", "mem_1", "mem_2", "cell")
    )
    in_specs = (P(MEM, None, "cell"), P("cell", MEM), P("cell", MEM), P("cell", MEM))
    out_specs = P(MEM, None, "cell")
    return jax.shard_map(local, mesh=torus, in_specs=in_specs, out_specs=out_specs, check_vma=False)
```

```python
import functools
import math

import jax
import jax.numpy as jnp
from jax import lax
from jax.experimental import pallas as pl
from jax.experimental.pallas import tpu as pltpu
from jax.sharding import Mesh
from jax.sharding import PartitionSpec as P

NS_ITERS = 8
MEM = ("mem_0", "mem_1", "mem_2")
PLANE = ("mem_0", "mem_1")
F32 = jnp.float32
BF16 = jnp.bfloat16
VMEM = pl.BlockSpec(memory_space=pltpu.VMEM)
HBM = pl.BlockSpec(memory_space=pltpu.HBM)
SMEM = pl.BlockSpec(memory_space=pltpu.SMEM)


def pack_kernel(x_ref, o_ref, buffer, sem, packed, sent):
    parts, width = buffer.shape[0], o_ref.shape[3]
    span = buffer.shape[3]
    each = span // width
    copies = [
        pltpu.make_async_copy(x_ref.at[:, :, pl.ds(i * span, span)], buffer.at[i], sem.at[i])
        for i in range(parts)
    ]
    for c in copies:
        c.start()
    results = [
        pltpu.make_async_copy(
            packed.at[pl.ds(i * each, each)], o_ref.at[pl.ds(i * each, each)], sent.at[i]
        )
        for i in range(parts)
    ]
    for i in range(parts):
        copies[i].wait()
        for k in range(each):
            block = buffer[i, :, :, k * width : (k + 1) * width]
            packed[i * each + k] = jnp.transpose(block, (1, 0, 2))
        results[i].start()
    for c in results:
        c.wait()


def unpack_kernel(y_ref, o_ref, buffer, sem):
    parts, width = buffer.shape[0], y_ref.shape[3]
    span = buffer.shape[3]
    each = span // width
    copies = []
    for i in range(parts):
        for k in range(each):
            block = jnp.transpose(y_ref[i * each + k], (1, 0, 2))
            buffer[i, :, :, k * width : (k + 1) * width] = block
        copy = pltpu.make_async_copy(
            buffer.at[i], o_ref.at[:, :, pl.ds(i * span, span)], sem.at[i]
        )
        copy.start()
        copies.append(copy)
    for c in copies:
        c.wait()


def tiles_of(members):
    blocks = members // 128
    return [
        (row * 128 + i * 8, column * 128)
        for row in range(blocks)
        for column in range(row, blocks)
        for i in range(16)
    ]


def rows_of(x_ref, f):
    groups, _, rows, width = x_ref.shape
    return x_ref[:, f].reshape(groups * rows, width)


def contract(a, b, dims):
    return lax.dot_general(a, b, (dims, ((), ())), preferred_element_type=F32)


def gram_kernel(
    core_ref, start_ref, location_ref, datum_ref, spread_ref, x_ref, keep_ref, send_ref, sum_ref, *, sites
):
    groups, fields, rows, width = x_ref.shape
    members = groups * rows
    norm_factor = math.sqrt(members - 1)
    scaled_parts, innovation_parts = [], []
    iota = lax.broadcasted_iota(jnp.int32, (width, 256), 0)

    def pair(ref, r):
        return jnp.concatenate([ref[r : r + 1, :], ref[r + 1 : r + 2, :]], axis=1)

    start = start_ref[0]
    for r in range(0, location_ref.shape[0], 2):
        location = pair(location_ref, r)
        picked = None
        for f in range(fields):
            chosen = jnp.where(iota == location - (start + f * sites), 1.0, 0.0).astype(BF16)
            term = contract(rows_of(x_ref, f), chosen, ((1,), (0,)))
            picked = term if picked is None else picked + term
        mean = jnp.sum(picked, axis=0, keepdims=True) / members
        anomaly = (picked - mean).astype(BF16).astype(F32)
        error = pair(spread_ref, r)
        scaled_parts.append((anomaly * (1.0 / (error * norm_factor))).astype(BF16))
        innovation_parts.append(((pair(datum_ref, r) - mean) / error).astype(BF16))
    scaled = jnp.concatenate(scaled_parts, axis=1)
    innovation = jnp.concatenate(innovation_parts, axis=1).astype(F32)
    innovation = jnp.broadcast_to(innovation, (16, innovation.shape[1])).astype(BF16)
    gram = contract(scaled, scaled, ((1,), (1,)))
    projected = contract(innovation, scaled, ((1,), (1,)))
    tiles = tiles_of(members)
    for t, (row, column) in enumerate(tiles):
        sum_ref[t] = gram[row : row + 8, column : column + 128]
    rows = jnp.concatenate(
        [projected[0:1, j * 128 : (j + 1) * 128] for j in range(members // 128)], axis=0
    )
    rows = jnp.concatenate([rows, pltpu.roll(rows, 64, 1)], axis=0)
    low_lanes = lax.broadcasted_iota(jnp.int32, rows.shape, 1) < 64
    sum_ref[len(tiles) - 1] = jnp.where(low_lanes, rows, sum_ref[len(tiles) - 1])
    core = core_ref[0]
    half = keep_ref.shape[0]
    keep_ref[...] = sum_ref[pl.ds(core * half, half)]
    send_ref[...] = sum_ref[pl.ds((1 - core) * half, half)]


def mean_kernel(x_ref, anomalies_ref, mean_ref):
    groups, fields, rows, width = x_ref.shape
    members = groups * rows
    for f in range(fields):
        x = x_ref[:, f].astype(F32)
        mean = jnp.sum(jnp.sum(x, axis=0), axis=0, keepdims=True) / members
        mean_ref[f : f + 1, :] = mean
        anomalies_ref[:, f] = (x - mean[None]).astype(BF16)


def halves(a):
    high = a.astype(BF16)
    return high, (a - high.astype(F32)).astype(BF16)


def thirds(row):
    high = row.astype(BF16).astype(F32)
    rest = row - high
    middle = rest.astype(BF16).astype(F32)
    low = rest - middle
    pad = jnp.zeros((13, row.shape[1]), F32)
    return jnp.concatenate([high, middle, low, pad], axis=0).astype(BF16)


def product(a, b):
    size = a[0].shape[0]
    half = size // 2
    dims = ((1,), (0,))

    def block(r, c):
        ah, al = (m[r : r + half, :] for m in a)
        bh, bl = (m[:, c : c + half] for m in b)
        return contract(ah, bh, dims) + (contract(ah, bl, dims) + contract(al, bh, dims))

    return block(0, 0), block(0, half), block(half, half)


def keep_product(pair, blocks):
    high_ref, low_ref = pair
    half = high_ref.shape[0] // 2
    first, side, last = blocks
    places = ((0, 0, first), (0, half, side), (half, half, last), (half, 0, jnp.transpose(side)))
    for r, c, value in places:
        high, low = halves(value)
        high_ref[r : r + half, c : c + half] = high
        low_ref[r : r + half, c : c + half] = low


def diagonal_of(size):
    rows = lax.broadcasted_iota(jnp.int32, (size, size), 0)
    return rows == lax.broadcasted_iota(jnp.int32, (size, size), 1)


def through(row, pair):
    parts = thirds(row)
    dims = ((1,), (0,))
    sent = contract(parts, pair[0][...], dims) + contract(parts, pair[1][...], dims)
    return jnp.sum(sent, axis=0, keepdims=True)


def keep_step(rest_ref, scale_ref, blocks):
    half = rest_ref.shape[0] // 2
    first, side, last = blocks
    diagonal = diagonal_of(half)
    for start, value in ((0, first), (half, last)):
        value = jnp.where(diagonal, 1.5, 0.0) - 0.5 * value
        scale = jnp.sum(jnp.where(diagonal, value, 0.0), axis=1, keepdims=True)
        scale_ref[start : start + half, :] = jnp.broadcast_to(scale, (half, scale_ref.shape[1]))
        rest = jnp.where(diagonal, 0.0, value).astype(BF16)
        rest_ref[start : start + half, start : start + half] = rest
    side = -0.5 * side
    rest_ref[:half, half:] = side.astype(BF16)
    rest_ref[half:, :half] = jnp.transpose(side).astype(BF16)


def stepped(rest_ref, scale_ref, pair):
    half = rest_ref.shape[0] // 2
    high_ref, low_ref = pair
    dims = ((1,), (0,))

    def block(r, c):
        rows, columns = slice(r, r + half), slice(c, c + half)
        scale = scale_ref[rows, :]
        scale = jnp.concatenate([scale] * (half // scale.shape[1]), axis=1)
        value = high_ref[rows, columns].astype(F32) + low_ref[rows, columns].astype(F32)
        rest = rest_ref[rows, :]
        moved = contract(rest, high_ref[:, columns], dims) + contract(rest, low_ref[:, columns], dims)
        return scale * value + moved

    return block(0, 0), block(0, half), block(half, half)


def analysis_kernel(
    core_ref,
    own_ref,
    other_ref,
    anomalies_ref,
    mean_ref,
    o_ref,
    sum_ref,
    sys_ref,
    yh,
    yl,
    zh,
    zl,
    th,
    tl,
    scale_ref,
):
    members = sys_ref.shape[0]
    norm_factor = math.sqrt(members - 1)
    blocks = members // 128
    core = core_ref[0]
    half = own_ref.shape[0]
    sum_ref[pl.ds(core * half, half)] = own_ref[...]
    sum_ref[pl.ds((1 - core) * half, half)] = other_ref[...]
    tiles = tiles_of(members)
    for t, (row, column) in enumerate(tiles):
        sys_ref[row : row + 8, column : column + 128] = sum_ref[t]
    tile = sum_ref[len(tiles) - 1]
    low_lanes = lax.broadcasted_iota(jnp.int32, (blocks, 128), 1) < 64
    projected = jnp.where(low_lanes, tile[0:blocks], pltpu.roll(tile[blocks : 2 * blocks], 64, 1))
    projected = jnp.concatenate([projected[j : j + 1, :] for j in range(blocks)], axis=1)
    corner = sys_ref[members - 128 :, members - 128 :]
    low_lanes = lax.broadcasted_iota(jnp.int32, tile.shape, 1) < 64
    sys_ref[members - 8 :, members - 128 :] = jnp.where(low_lanes, jnp.transpose(corner)[120:128], tile)
    squares = jnp.zeros((128, 128), F32)
    unit = jnp.where(diagonal_of(128), 1.0, 0.0)
    for i in range(blocks):
        here = slice(i * 128, i * 128 + 128)
        value = sys_ref[here, here] + unit
        sys_ref[here, here] = value
        squares = squares + value * value
        for j in range(i + 1, blocks):
            there = slice(j * 128, j * 128 + 128)
            value = sys_ref[here, there]
            sys_ref[there, here] = jnp.transpose(value)
            squares = squares + 2.0 * (value * value)
    squares = jnp.sum(jnp.sum(squares, axis=0, keepdims=True), axis=1, keepdims=True)
    norm_scale = jnp.sqrt(squares)
    one_over = 1.0 / norm_scale
    half_size = members // 2
    half_diagonal = diagonal_of(half_size)
    y, z, t = (yh, yl), (zh, zl), (th, tl)

    for r in (0, half_size):
        for c in (0, half_size):
            here = (slice(r, r + half_size), slice(c, c + half_size))
            value = sys_ref[here] * one_over
            th[here], tl[here] = halves(value)
            base = jnp.where(half_diagonal, 1.5, 0.0) if r == c else 0.0
            zh[here], zl[here] = halves(base - 0.5 * value)
    keep_product(y, product(z, t))

    def turn(_, carry):
        keep_step(th, scale_ref, product(z, y))
        next_y, next_z = stepped(th, scale_ref, y), stepped(th, scale_ref, z)
        keep_product(y, next_y)
        keep_product(z, next_z)
        return carry

    lax.fori_loop(0, NS_ITERS - 2, turn, 0, unroll=NS_ITERS - 2)
    keep_step(th, scale_ref, product(z, y))
    first, side, last = stepped(th, scale_ref, z)
    sys_ref[:half_size, :half_size] = first
    sys_ref[:half_size, half_size:] = side
    sys_ref[half_size:, half_size:] = last
    sys_ref[half_size:, :half_size] = jnp.transpose(side)
    iterate_z = sys_ref[...]
    root = jnp.sqrt(norm_scale)
    dims = ((1,), (0,))
    zs = halves(iterate_z)
    three = thirds(projected)
    sent = contract(three, zs[0], dims) + contract(three, zs[1], dims)
    shift = jnp.sum(sent, axis=0, keepdims=True) / (root * norm_factor)
    weights = (iterate_z * (1.0 / root)).astype(BF16)
    combined = jnp.sum(contract(thirds(shift), weights, dims), axis=0, keepdims=True)
    combined = thirds(combined)
    groups, fields, rows, width = anomalies_ref.shape
    for f in range(fields):
        anomalies = rows_of(anomalies_ref, f)
        mean_shift = jnp.sum(contract(combined, anomalies, dims), axis=0, keepdims=True)
        base = mean_ref[f : f + 1, :] + mean_shift
        updated = contract(weights, anomalies, dims)
        o_ref[:, f] = (base + updated).astype(BF16).reshape(groups, rows, width)


def far(a):
    return pltpu.with_memory_space_constraint(a, pltpu.HBM)


def near(a):
    return pltpu.with_memory_space_constraint(a, pltpu.VMEM)


def spread(part, peers):
    return jnp.broadcast_to(part[None], (peers, *part.shape)).reshape(-1, *part.shape[1:])


def summed(part, peers):
    return jnp.sum(part.reshape(peers, -1, *part.shape[1:]), axis=0)


def local(prior_ensemble, measurement_location, measurement_datum, measurement_spread):
    rows, fields, span = prior_ensemble.shape
    peers = lax.axis_size(MEM)
    members = rows * peers
    width = span // peers
    core = lax.axis_index("mem_2").reshape(1).astype(jnp.int32)
    parts = 4
    staging = [pltpu.VMEM((parts, rows, fields, span // parts), BF16), pltpu.SemaphoreType.DMA((parts,))]
    tiled = pltpu.VMEM((peers, fields, rows, width), BF16)
    packed = pl.pallas_call(
        pack_kernel,
        out_shape=pltpu.HBM(tiled.shape, BF16),
        in_specs=[HBM],
        out_specs=HBM,
        scratch_shapes=staging + [tiled, pltpu.SemaphoreType.DMA((parts,))],
        compiler_params=pltpu.CompilerParams(vmem_limit_bytes=8 << 20),
        name="pack",
    )(far(prior_ensemble))
    sites = span * lax.axis_size("cell")
    block_start = (lax.axis_index("cell") * peers + lax.axis_index(MEM)) * width
    block_start = block_start.reshape(1).astype(jnp.int32)
    packed, core, block_start = lax.optimization_barrier((packed, core, block_start))
    state = near(lax.all_to_all(packed, MEM, 0, 0, tiled=True))
    plane = lax.axis_size(PLANE)
    share = -(-len(tiles_of(members)) // (2 * plane))
    half = pltpu.VMEM((share * plane, 8, 128), F32)
    both = pltpu.VMEM((2 * share * plane, 8, 128), F32)
    keep, send = pl.pallas_call(
        functools.partial(gram_kernel, sites=sites),
        out_shape=(half, half),
        in_specs=[SMEM, SMEM, VMEM, VMEM, VMEM, VMEM],
        out_specs=(VMEM, VMEM),
        scratch_shapes=[both],
        compiler_params=pltpu.CompilerParams(vmem_limit_bytes=24 << 20),
        name="gram",
    )(core, block_start, measurement_location, measurement_datum, measurement_spread, state)
    swap = [(0, 1), (1, 0)]
    part = keep + lax.ppermute(send, "mem_2", swap)
    part = lax.all_to_all(part, PLANE, 0, 0, tiled=True)
    part = summed(part, plane)
    planes = lax.axis_size("cell")
    part = summed(lax.all_to_all(spread(part, planes), "cell", 0, 0, tiled=True), planes)
    anomalies, mean = pl.pallas_call(
        mean_kernel,
        out_shape=(tiled, pltpu.VMEM((fields, width), F32)),
        input_output_aliases={0: 0},
        in_specs=[VMEM],
        out_specs=(VMEM, VMEM),
        compiler_params=pltpu.CompilerParams(vmem_limit_bytes=24 << 20),
        name="mean",
    )(state)
    own = lax.all_to_all(spread(part, plane), PLANE, 0, 0, tiled=True)
    other = lax.ppermute(own, "mem_2", swap)
    square = pltpu.VMEM((members, members), BF16)
    whole = pltpu.VMEM((members, members), F32)
    analysis = pl.pallas_call(
        analysis_kernel,
        out_shape=tiled,
        in_specs=[SMEM, VMEM, VMEM, VMEM, VMEM],
        out_specs=VMEM,
        scratch_shapes=[both, whole] + [square] * 6 + [pltpu.VMEM((members, 128), F32)],
        compiler_params=pltpu.CompilerParams(vmem_limit_bytes=32 << 20),
        name="analysis",
    )(core, near(own), near(other), near(anomalies), near(mean))
    returned = lax.all_to_all(analysis, MEM, 0, 0, tiled=True)
    return pl.pallas_call(
        unpack_kernel,
        out_shape=jax.ShapeDtypeStruct(prior_ensemble.shape, BF16),
        in_specs=[VMEM],
        out_specs=HBM,
        scratch_shapes=staging,
        compiler_params=pltpu.CompilerParams(vmem_limit_bytes=8 << 20),
        name="unpack",
    )(near(returned))


def solution(mesh):
    torus = Mesh(
        mesh.devices.reshape(4, 4, 2, mesh.shape["cell"]), ("mem_0", "mem_1", "mem_2", "cell")
    )
    in_specs = (P(MEM, None, "cell"), P("cell", MEM), P("cell", MEM), P("cell", MEM))
    out_specs = P(MEM, None, "cell")
    return jax.shard_map(local, mesh=torus, in_specs=in_specs, out_specs=out_specs, check_vma=False)
```

```python
import functools
import math

import jax
import jax.numpy as jnp
from jax import lax
from jax.experimental import pallas as pl
from jax.experimental.pallas import tpu as pltpu
from jax.sharding import Mesh
from jax.sharding import PartitionSpec as P

NS_ITERS = 8
MEM = ("mem_0", "mem_1", "mem_2")
PLANE = ("mem_0", "mem_1")
F32 = jnp.float32
BF16 = jnp.bfloat16
VMEM = pl.BlockSpec(memory_space=pltpu.VMEM)
HBM = pl.BlockSpec(memory_space=pltpu.HBM)
SMEM = pl.BlockSpec(memory_space=pltpu.SMEM)


def pack_kernel(x_ref, o_ref, buffer, sem, packed, sent):
    parts, width = buffer.shape[0], o_ref.shape[3]
    span = buffer.shape[3]
    each = span // width
    copies = [
        pltpu.make_async_copy(x_ref.at[:, :, pl.ds(i * span, span)], buffer.at[i], sem.at[i])
        for i in range(parts)
    ]
    for c in copies:
        c.start()
    results = [
        pltpu.make_async_copy(
            packed.at[pl.ds(i * each, each)], o_ref.at[pl.ds(i * each, each)], sent.at[i]
        )
        for i in range(parts)
    ]
    for i in range(parts):
        copies[i].wait()
        for k in range(each):
            block = buffer[i, :, :, k * width : (k + 1) * width]
            packed[i * each + k] = jnp.transpose(block, (1, 0, 2))
        results[i].start()
    for c in results:
        c.wait()


def unpack_kernel(y_ref, o_ref, buffer, sem):
    parts, width = buffer.shape[0], y_ref.shape[3]
    span = buffer.shape[3]
    each = span // width
    copies = []
    for i in range(parts):
        for k in range(each):
            block = jnp.transpose(y_ref[i * each + k], (1, 0, 2))
            buffer[i, :, :, k * width : (k + 1) * width] = block
        copy = pltpu.make_async_copy(
            buffer.at[i], o_ref.at[:, :, pl.ds(i * span, span)], sem.at[i]
        )
        copy.start()
        copies.append(copy)
    for c in copies:
        c.wait()


def tiles_of(members):
    blocks = members // 128
    return [
        (row * 128 + i * 8, column * 128)
        for row in range(blocks)
        for column in range(row, blocks)
        for i in range(16)
    ]


def rows_of(x_ref, f):
    groups, _, rows, width = x_ref.shape
    return x_ref[:, f].reshape(groups * rows, width)


def contract(a, b, dims):
    return lax.dot_general(a, b, (dims, ((), ())), preferred_element_type=F32)


def gram_kernel(
    core_ref, start_ref, location_ref, datum_ref, spread_ref, x_ref, keep_ref, send_ref, sum_ref, *, sites
):
    groups, fields, rows, width = x_ref.shape
    members = groups * rows
    norm_factor = math.sqrt(members - 1)
    scaled_parts, innovation_parts = [], []
    iota = lax.broadcasted_iota(jnp.int32, (width, 256), 0)

    def pair(ref, r):
        return jnp.concatenate([ref[r : r + 1, :], ref[r + 1 : r + 2, :]], axis=1)

    start = start_ref[0]
    for r in range(0, location_ref.shape[0], 2):
        location = pair(location_ref, r)
        picked = None
        for f in range(fields):
            chosen = jnp.where(iota == location - (start + f * sites), 1.0, 0.0).astype(BF16)
            term = contract(rows_of(x_ref, f), chosen, ((1,), (0,)))
            picked = term if picked is None else picked + term
        mean = jnp.sum(picked, axis=0, keepdims=True) / members
        anomaly = (picked - mean).astype(BF16).astype(F32)
        error = pair(spread_ref, r)
        scaled_parts.append((anomaly * (1.0 / (error * norm_factor))).astype(BF16))
        innovation_parts.append(((pair(datum_ref, r) - mean) / error).astype(BF16))
    scaled = jnp.concatenate(scaled_parts, axis=1)
    innovation = jnp.concatenate(innovation_parts, axis=1).astype(F32)
    innovation = jnp.broadcast_to(innovation, (16, innovation.shape[1])).astype(BF16)
    gram = contract(scaled, scaled, ((1,), (1,)))
    projected = contract(innovation, scaled, ((1,), (1,)))
    tiles = tiles_of(members)
    for t, (row, column) in enumerate(tiles):
        sum_ref[t] = gram[row : row + 8, column : column + 128]
    rows = jnp.concatenate(
        [projected[0:1, j * 128 : (j + 1) * 128] for j in range(members // 128)], axis=0
    )
    rows = jnp.concatenate([rows, pltpu.roll(rows, 64, 1)], axis=0)
    low_lanes = lax.broadcasted_iota(jnp.int32, rows.shape, 1) < 64
    sum_ref[len(tiles) - 1] = jnp.where(low_lanes, rows, sum_ref[len(tiles) - 1])
    core = core_ref[0]
    half = keep_ref.shape[0]
    keep_ref[...] = sum_ref[pl.ds(core * half, half)]
    send_ref[...] = sum_ref[pl.ds((1 - core) * half, half)]


def mean_kernel(x_ref, anomalies_ref, mean_ref):
    groups, fields, rows, width = x_ref.shape
    members = groups * rows
    for f in range(fields):
        x = x_ref[:, f].astype(F32)
        mean = jnp.sum(jnp.sum(x, axis=0), axis=0, keepdims=True) / members
        mean_ref[f : f + 1, :] = mean
        anomalies_ref[:, f] = (x - mean[None]).astype(BF16)


def halves(a):
    high = a.astype(BF16)
    return high, (a - high.astype(F32)).astype(BF16)


def thirds(row):
    high = row.astype(BF16).astype(F32)
    rest = row - high
    middle = rest.astype(BF16).astype(F32)
    low = rest - middle
    pad = jnp.zeros((13, row.shape[1]), F32)
    return jnp.concatenate([high, middle, low, pad], axis=0).astype(BF16)


def product(a, b):
    size = a[0].shape[0]
    half = size // 2
    dims = ((1,), (0,))

    def block(r, c):
        ah, al = (m[r : r + half, :] for m in a)
        bh, bl = (m[:, c : c + half] for m in b)
        return contract(ah, bh, dims) + (contract(ah, bl, dims) + contract(al, bh, dims))

    return block(0, 0), block(0, half), block(half, half)


def keep_product(pair, blocks):
    high_ref, low_ref = pair
    half = high_ref.shape[0] // 2
    first, side, last = blocks
    places = ((0, 0, first), (0, half, side), (half, half, last), (half, 0, jnp.transpose(side)))
    for r, c, value in places:
        high, low = halves(value)
        high_ref[r : r + half, c : c + half] = high
        low_ref[r : r + half, c : c + half] = low


def diagonal_of(size):
    rows = lax.broadcasted_iota(jnp.int32, (size, size), 0)
    return rows == lax.broadcasted_iota(jnp.int32, (size, size), 1)


def through(row, pair):
    parts = thirds(row)
    dims = ((1,), (0,))
    sent = contract(parts, pair[0][...], dims) + contract(parts, pair[1][...], dims)
    return jnp.sum(sent, axis=0, keepdims=True)


def keep_step(rest_ref, scale_ref, blocks):
    half = rest_ref.shape[0] // 2
    first, side, last = blocks
    diagonal = diagonal_of(half)
    for start, value in ((0, first), (half, last)):
        value = jnp.where(diagonal, 1.5, 0.0) - 0.5 * value
        scale = jnp.sum(jnp.where(diagonal, value, 0.0), axis=1, keepdims=True)
        scale_ref[start : start + half, :] = jnp.broadcast_to(scale, (half, scale_ref.shape[1]))
        rest = jnp.where(diagonal, 0.0, value).astype(BF16)
        rest_ref[start : start + half, start : start + half] = rest
    side = -0.5 * side
    rest_ref[:half, half:] = side.astype(BF16)
    rest_ref[half:, :half] = jnp.transpose(side).astype(BF16)


def stepped(rest_ref, scale_ref, pair):
    half = rest_ref.shape[0] // 2
    high_ref, low_ref = pair
    dims = ((1,), (0,))

    def block(r, c):
        rows, columns = slice(r, r + half), slice(c, c + half)
        scale = scale_ref[rows, :]
        scale = jnp.concatenate([scale] * (half // scale.shape[1]), axis=1)
        value = high_ref[rows, columns].astype(F32) + low_ref[rows, columns].astype(F32)
        rest = rest_ref[rows, :]
        moved = contract(rest, high_ref[:, columns], dims) + contract(rest, low_ref[:, columns], dims)
        return scale * value + moved

    return block(0, 0), block(0, half), block(half, half)


def analysis_kernel(
    core_ref,
    own_ref,
    other_ref,
    anomalies_ref,
    mean_ref,
    o_ref,
    sum_ref,
    sys_ref,
    yh,
    yl,
    zh,
    zl,
    th,
    tl,
    scale_ref,
):
    members = sys_ref.shape[0]
    norm_factor = math.sqrt(members - 1)
    blocks = members // 128
    core = core_ref[0]
    half = own_ref.shape[0]
    sum_ref[pl.ds(core * half, half)] = own_ref[...]
    sum_ref[pl.ds((1 - core) * half, half)] = other_ref[...]
    tiles = tiles_of(members)
    for t, (row, column) in enumerate(tiles):
        sys_ref[row : row + 8, column : column + 128] = sum_ref[t]
    tile = sum_ref[len(tiles) - 1]
    low_lanes = lax.broadcasted_iota(jnp.int32, (blocks, 128), 1) < 64
    projected = jnp.where(low_lanes, tile[0:blocks], pltpu.roll(tile[blocks : 2 * blocks], 64, 1))
    projected = jnp.concatenate([projected[j : j + 1, :] for j in range(blocks)], axis=1)
    corner = sys_ref[members - 128 :, members - 128 :]
    low_lanes = lax.broadcasted_iota(jnp.int32, tile.shape, 1) < 64
    sys_ref[members - 8 :, members - 128 :] = jnp.where(low_lanes, jnp.transpose(corner)[120:128], tile)
    squares = jnp.zeros((128, 128), F32)
    unit = jnp.where(diagonal_of(128), 1.0, 0.0)
    for i in range(blocks):
        here = slice(i * 128, i * 128 + 128)
        value = sys_ref[here, here] + unit
        sys_ref[here, here] = value
        squares = squares + value * value
        for j in range(i + 1, blocks):
            there = slice(j * 128, j * 128 + 128)
            value = sys_ref[here, there]
            sys_ref[there, here] = jnp.transpose(value)
            squares = squares + 2.0 * (value * value)
    squares = jnp.sum(jnp.sum(squares, axis=0, keepdims=True), axis=1, keepdims=True)
    norm_scale = jnp.sqrt(squares)
    one_over = 1.0 / norm_scale
    half_size = members // 2
    half_diagonal = diagonal_of(half_size)
    y, z, t = (yh, yl), (zh, zl), (th, tl)

    for r in (0, half_size):
        for c in (0, half_size):
            here = (slice(r, r + half_size), slice(c, c + half_size))
            value = sys_ref[here] * one_over
            th[here], tl[here] = halves(value)
            base = jnp.where(half_diagonal, 1.5, 0.0) if r == c else 0.0
            zh[here], zl[here] = halves(base - 0.5 * value)
    keep_product(y, product(z, t))

    def turn(_, carry):
        keep_step(th, scale_ref, product(z, y))
        next_y, next_z = stepped(th, scale_ref, y), stepped(th, scale_ref, z)
        keep_product(y, next_y)
        keep_product(z, next_z)
        return carry

    lax.fori_loop(0, NS_ITERS - 2, turn, 0, unroll=NS_ITERS - 2)
    keep_step(th, scale_ref, product(z, y))
    first, side, last = stepped(th, scale_ref, z)
    sys_ref[:half_size, :half_size] = first
    sys_ref[:half_size, half_size:] = side
    sys_ref[half_size:, half_size:] = last
    sys_ref[half_size:, :half_size] = jnp.transpose(side)
    iterate_z = sys_ref[...]
    root = jnp.sqrt(norm_scale)
    dims = ((1,), (0,))
    zs = halves(iterate_z)
    three = thirds(projected)
    sent = contract(three, zs[0], dims) + contract(three, zs[1], dims)
    shift = jnp.sum(sent, axis=0, keepdims=True) / (root * norm_factor)
    weights = (iterate_z * (1.0 / root)).astype(BF16)
    combined = jnp.sum(contract(thirds(shift), weights, dims), axis=0, keepdims=True)
    combined = thirds(combined)
    weights = jnp.concatenate([combined, weights], axis=0)
    groups, fields, rows, width = anomalies_ref.shape
    for f in range(fields):
        anomalies = rows_of(anomalies_ref, f)
        moved = contract(weights, anomalies, dims)
        extra = combined.shape[0]
        mean_shift = jnp.sum(moved[:extra], axis=0, keepdims=True)
        base = mean_ref[f : f + 1, :] + mean_shift
        o_ref[:, f] = (base + moved[extra:]).astype(BF16).reshape(groups, rows, width)


def far(a):
    return pltpu.with_memory_space_constraint(a, pltpu.HBM)


def near(a):
    return pltpu.with_memory_space_constraint(a, pltpu.VMEM)


def spread(part, peers):
    return jnp.broadcast_to(part[None], (peers, *part.shape)).reshape(-1, *part.shape[1:])


def summed(part, peers):
    return jnp.sum(part.reshape(peers, -1, *part.shape[1:]), axis=0)


def local(prior_ensemble, measurement_location, measurement_datum, measurement_spread):
    rows, fields, span = prior_ensemble.shape
    peers = lax.axis_size(MEM)
    members = rows * peers
    width = span // peers
    core = lax.axis_index("mem_2").reshape(1).astype(jnp.int32)
    parts = 8
    staging = [pltpu.VMEM((parts, rows, fields, span // parts), BF16), pltpu.SemaphoreType.DMA((parts,))]
    tiled = pltpu.VMEM((peers, fields, rows, width), BF16)
    packed = pl.pallas_call(
        pack_kernel,
        out_shape=pltpu.HBM(tiled.shape, BF16),
        in_specs=[HBM],
        out_specs=HBM,
        scratch_shapes=staging + [tiled, pltpu.SemaphoreType.DMA((parts,))],
        compiler_params=pltpu.CompilerParams(vmem_limit_bytes=8 << 20),
        name="pack",
    )(far(prior_ensemble))
    sites = span * lax.axis_size("cell")
    block_start = (lax.axis_index("cell") * peers + lax.axis_index(MEM)) * width
    block_start = block_start.reshape(1).astype(jnp.int32)
    packed, core, block_start = lax.optimization_barrier((packed, core, block_start))
    state = near(lax.all_to_all(packed, MEM, 0, 0, tiled=True))
    plane = lax.axis_size(PLANE)
    share = -(-len(tiles_of(members)) // (2 * plane))
    half = pltpu.VMEM((share * plane, 8, 128), F32)
    both = pltpu.VMEM((2 * share * plane, 8, 128), F32)
    keep, send = pl.pallas_call(
        functools.partial(gram_kernel, sites=sites),
        out_shape=(half, half),
        in_specs=[SMEM, SMEM, VMEM, VMEM, VMEM, VMEM],
        out_specs=(VMEM, VMEM),
        scratch_shapes=[both],
        compiler_params=pltpu.CompilerParams(vmem_limit_bytes=24 << 20),
        name="gram",
    )(core, block_start, measurement_location, measurement_datum, measurement_spread, state)
    swap = [(0, 1), (1, 0)]
    part = keep + lax.ppermute(send, "mem_2", swap)
    part = lax.all_to_all(part, PLANE, 0, 0, tiled=True)
    part = summed(part, plane)
    planes = lax.axis_size("cell")
    part = summed(lax.all_to_all(spread(part, planes), "cell", 0, 0, tiled=True), planes)
    anomalies, mean = pl.pallas_call(
        mean_kernel,
        out_shape=(tiled, pltpu.VMEM((fields, width), F32)),
        input_output_aliases={0: 0},
        in_specs=[VMEM],
        out_specs=(VMEM, VMEM),
        compiler_params=pltpu.CompilerParams(vmem_limit_bytes=24 << 20),
        name="mean",
    )(state)
    own = lax.all_to_all(spread(part, plane), PLANE, 0, 0, tiled=True)
    other = lax.ppermute(own, "mem_2", swap)
    square = pltpu.VMEM((members, members), BF16)
    whole = pltpu.VMEM((members, members), F32)
    analysis = pl.pallas_call(
        analysis_kernel,
        out_shape=tiled,
        in_specs=[SMEM, VMEM, VMEM, VMEM, VMEM],
        out_specs=VMEM,
        scratch_shapes=[both, whole] + [square] * 6 + [pltpu.VMEM((members, 128), F32)],
        compiler_params=pltpu.CompilerParams(vmem_limit_bytes=32 << 20),
        name="analysis",
    )(core, near(own), near(other), near(anomalies), near(mean))
    returned = lax.all_to_all(analysis, MEM, 0, 0, tiled=True)
    return pl.pallas_call(
        unpack_kernel,
        out_shape=jax.ShapeDtypeStruct(prior_ensemble.shape, BF16),
        in_specs=[VMEM],
        out_specs=HBM,
        scratch_shapes=staging,
        compiler_params=pltpu.CompilerParams(vmem_limit_bytes=8 << 20),
        name="unpack",
    )(near(returned))


def solution(mesh):
    torus = Mesh(
        mesh.devices.reshape(4, 4, 2, mesh.shape["cell"]), ("mem_0", "mem_1", "mem_2", "cell")
    )
    in_specs = (P(MEM, None, "cell"), P("cell", MEM), P("cell", MEM), P("cell", MEM))
    out_specs = P(MEM, None, "cell")
    return jax.shard_map(local, mesh=torus, in_specs=in_specs, out_specs=out_specs, check_vma=False)
```
